32 devices in a mesh: dp: 4 (over x, core), section: 2 (over y), tensor: 4 (over z).
Axes of the slice: x: 2, y: 2, z: 4, core: 2. Of those that a mesh axis runs over, the one named last changes fastest.
Arguments:
- section_input: bfloat16 [2, 512, 3072], P('section', 'dp'), may hold values from -6 to 6
- norm_gain: float32 [2, 3072], P('section'), may hold values from 0.25 to 1.75
- value_weight: bfloat16 [2, 1536, 3072], P('section', 'tensor'), may hold values from -0.109375 to 0.109375
- attn_probs: bfloat16 [2, 12, 512, 128], P('section', 'tensor', 'dp'), may hold values from 0 to 1, as said below
- out_weight: bfloat16 [2, 3072, 1536], P('section', None, 'tensor'), may hold values from -0.15625 to 0.15625
- direction: bfloat16 [2, 3072, 1536], P('section', None, 'tensor'), may hold values from -0.15625 to 0.15625
- curvature: bfloat16 [512, 3072], P('dp'), may hold values from 0.19921875 to 2
Outputs:
- curvature_product: float32 [2, 3072, 1536], P('section', 'dp', 'tensor')
The draws below stay inside these ranges and needn't reach their ends.
Inputs may be any that keep to these rules, and one draw needn't show every extreme that they name: `attn_probs`: each row is a causal attention distribution over the 128 tokens of its sequence: nonnegative, summing to one up to rounding, zero for keys after the query's position in the sequence.
All inputs are finite; a program needn't handle non-finite values.
Results may differ from the reference program's by a relative error of at most 0.013.
Values may be sent and summed in bfloat16 or wider, within the bound.
A program may use at most 64 MiB of HBM per device.

```python
import math
import jax
import jax.numpy as jnp
from jax import lax

D = 3072
HEAD_DIM = 128
TOK_DEV = 128
HEADS = 12
SECTIONS = 2
TOKENS = 512
N_DP = 4


def draw_attn_probs(key, part):
    shape = (SECTIONS, HEADS, TOKENS, TOK_DEV)
    logits = 1.5 * jax.random.normal(key, shape, jnp.float32)
    query = (jnp.arange(TOKENS, dtype=jnp.int32) % TOK_DEV)[:, None]
    keypos = jnp.arange(TOK_DEV, dtype=jnp.int32)[None, :]
    allowed = keypos <= query
    weights = jnp.where(allowed, jnp.exp(logits), 0.0)
    probs = weights / jnp.sum(weights, axis=-1, keepdims=True)
    return probs.astype(jnp.bfloat16)


def shard_levels(rng, shape, pieces, smallest, high):
    factor_of, own = 1.0, jax.random.fold_in(rng, 6)
    for dim, shards_of in pieces:
        heights = jnp.exp(jax.random.uniform(jax.random.fold_in(own, dim), (shards_of,), jnp.float32, smallest / len(pieces), high / len(pieces)))
        factor_of = factor_of * jnp.repeat(heights, shape[dim] // shards_of).reshape([-1 if axis == dim else 1 for axis in range(len(shape))])
    return factor_of


def gaussian(key, dims, deviation, most, split=(), kind=jnp.bfloat16):
    values = jax.random.normal(key, dims, jnp.float32) * deviation
    if len(split) > 0:
        values = shard_levels(key, dims, split, -0.22, 0.18) * values
    return jnp.clip(values, min=-most, max=most).astype(kind)


def setup_inputs(seed: int = 0) -> dict:
    key_list = jax.random.split(jax.random.key(seed), 8)
    section_input = gaussian(key_list[0], (SECTIONS, TOKENS, D), 1.0, 6.0, ((0, 2), (1, 4)))
    norm_gain = jnp.clip(1.0 + 0.15 * jax.random.normal(key_list[1], (SECTIONS, D), jnp.float32), 0.25, 1.75)
    value_weight = gaussian(key_list[2], (SECTIONS, HEADS * HEAD_DIM, D), D ** -0.5, 0.109375, ((0, 2), (1, 4)))
    attn_probs = draw_attn_probs(jax.random.fold_in(key_list[7], 71), 0)
    out_weight = gaussian(key_list[4], (SECTIONS, D, HEADS * HEAD_DIM), (HEADS * HEAD_DIM) ** -0.5, 0.15625, ((0, 2), (2, 4)))
    direction = gaussian(key_list[5], (SECTIONS, D, HEADS * HEAD_DIM), (HEADS * HEAD_DIM) ** -0.5, 0.15625, ((0, 2), (2, 4)))
    curvature = jnp.clip(jnp.exp(math.log(2.0) - 2.306499 * jax.random.uniform(key_list[6], (TOKENS, D), jnp.float32) ** shard_levels(key_list[6], (TOKENS, D), ((0, 4),), -0.2, 0.2)), 0.19921875, 2.0).astype(jnp.bfloat16)
    return {"section_input": section_input, "norm_gain": norm_gain, "value_weight": value_weight, "attn_probs": attn_probs, "out_weight": out_weight, "direction": direction, "curvature": curvature}


def mixing(probs, vals):
    wide = probs.astype(jnp.float32).reshape(HEADS, N_DP, TOK_DEV, TOK_DEV)
    cols = vals.astype(jnp.float32).reshape(N_DP, TOK_DEV, HEADS, HEAD_DIM)
    return jnp.einsum('hbqk,bkhd->bqhd', wide, cols).reshape(TOKENS, HEADS * HEAD_DIM)

def mixing_back(probs, grads):
    wide = probs.astype(jnp.float32).reshape(HEADS, N_DP, TOK_DEV, TOK_DEV)
    cols = grads.astype(jnp.float32).reshape(N_DP, TOK_DEV, HEADS, HEAD_DIM)
    return jnp.einsum('hbqk,bqhd->bkhd', wide, cols).reshape(TOKENS, HEADS * HEAD_DIM)

def reference(section_input, norm_gain, value_weight, attn_probs, out_weight, direction, curvature):
    saved = []
    tangent = jnp.zeros((TOKENS, D), jnp.bfloat16)
    for layer in range(SECTIONS):
        xval = section_input[layer].astype(jnp.float32)
        gain = norm_gain[layer]
        rnorm = lax.rsqrt(lax.optimization_barrier(jnp.mean(xval * xval, axis=-1, keepdims=True)) + 1e-06)
        normed = (xval * rnorm * gain).astype(jnp.bfloat16)
        values = jnp.dot(normed, value_weight[layer].T, preferred_element_type=jnp.float32).astype(jnp.bfloat16)
        act = mixing(attn_probs[layer], values).astype(jnp.bfloat16)
        tfloat = tangent.astype(jnp.float32)
        tnorm = (gain * (rnorm * tfloat - rnorm ** 3 * xval * lax.optimization_barrier(jnp.mean(xval * tfloat, axis=-1, keepdims=True)))).astype(jnp.bfloat16)
        tvals = jnp.dot(tnorm, value_weight[layer].T, preferred_element_type=jnp.float32).astype(jnp.bfloat16)
        tmix = mixing(attn_probs[layer], tvals).astype(jnp.bfloat16)
        total = jnp.dot(tmix, out_weight[layer].T, preferred_element_type=jnp.float32) + jnp.dot(act, direction[layer].T, preferred_element_type=jnp.float32)
        tangent = (tfloat + total).astype(jnp.bfloat16)
        saved.append((xval, gain, rnorm, act))
    adjoint = (curvature.astype(jnp.float32) * tangent.astype(jnp.float32)).astype(jnp.bfloat16)
    results = [None] * SECTIONS
    for layer in range(SECTIONS - 1, -1, -1):
        xval, gain, rnorm, act = saved[layer]
        results[layer] = jnp.dot(adjoint.T, act, preferred_element_type=jnp.float32)
        if layer > 0:
            gmix = jnp.dot(adjoint, out_weight[layer], preferred_element_type=jnp.float32)
            gvals = mixing_back(attn_probs[layer], gmix).astype(jnp.bfloat16)
            gnorm = jnp.dot(gvals, value_weight[layer], preferred_element_type=jnp.float32)
            gxval = rnorm * gain * gnorm - rnorm ** 3 * xval * lax.optimization_barrier(jnp.mean(xval * gain * gnorm, axis=-1, keepdims=True))
            adjoint = (adjoint.astype(jnp.float32) + gxval).astype(jnp.bfloat16)
    return jnp.stack(results)
```

```python
import functools

import jax
import jax.numpy as jnp
from jax import lax
from jax.experimental import pallas as pl
from jax.experimental.pallas import tpu as pltpu
from jax.sharding import PartitionSpec as P

MESH = pl.DeviceIdType.MESH
BF = jnp.bfloat16
F32 = jnp.float32


def dot_nt(a, b):
    return lax.dot_general(a, b, (((1,), (1,)), ((), ())), preferred_element_type=F32)


def dot_tn(a, b):
    return lax.dot_general(a, b, (((0,), (0,)), ((), ())), preferred_element_type=F32)


def dot_nn(a, b):
    return lax.dot_general(a, b, (((1,), (0,)), ((), ())), preferred_element_type=F32)


def kernel(
    fused, S, T, N,
    x_ref, gain_ref, probs_ref, wv_hbm, wd_hbm, wo_hbm, curv_hbm,
    *rest,
):
    if fused:
        prod_ref, rest = rest[0], rest[1:]
    else:
        gout_ref, actout_ref, rest = rest[0], rest[1], rest[2:]
    (
        wv, wd, wo, curv, act, part, partb, in_a, in_d, in_f, gpartb, normed, tn, gfull, trow, grow,
        actall, gall,
        load_sem, act_send, act_recv, a_send, a_recv, tn_send, tn_recv, d_send, d_recv,
        s_send, s_recv, f_send, f_recv, h_send, h_recv, x_send, x_recv,
    ) = rest
    d = lax.axis_index("dp")
    s = lax.axis_index("section")
    i = lax.axis_index("tensor")
    tok, width = x_ref.shape
    rows = tok // T
    heads = probs_ref.shape[0]
    hd = wv.shape[0] // heads
    feats = width // N
    CH = 512 if width % 512 == 0 else width
    chunks = [slice(c, c + CH) for c in range(0, width, CH)]

    def rows_at(j):
        return pl.ds(pl.multiple_of(j * rows, rows), rows)

    def feats_at(j):
        return pl.ds(pl.multiple_of(j * feats, 128), feats)

    def peer(me, k, n):
        return lax.rem(me + k, n)

    loads = [
        pltpu.make_async_copy(src, dst, load_sem.at[k])
        for k, (src, dst) in enumerate(((wv_hbm, wv), (wd_hbm, wd), (wo_hbm, wo), (curv_hbm, curv)))
    ]
    for copy in loads:
        copy.start()

    barrier = pltpu.get_barrier_semaphore()

    def greet(dev):
        pl.semaphore_signal(barrier, inc=1, device_id=dev, device_id_type=MESH)

    for k in range(1, T):
        greet({"dp": d, "section": s, "tensor": peer(i, k, T)})
    for k in range(1, N):
        greet({"dp": peer(d, k, N), "section": s, "tensor": i})
    for low in range(S - 1):
        wide = N if (fused and low == 0) else 1

        @pl.when(s == low)
        def _():
            for k in range(wide):
                for j in range(T):
                    greet({"dp": peer(d, k, N), "section": s + 1, "tensor": j})

        @pl.when(s == low + 1)
        def _():
            for k in range(wide):
                for j in range(T):
                    greet({"dp": peer(d, k, N), "section": s - 1, "tensor": j})

    gain = gain_ref[...]
    xf = x_ref[...].astype(F32)
    rnorm = lax.rsqrt(jnp.mean(xf * xf, axis=-1, keepdims=True) + 1e-06)
    normed[...] = (xf * rnorm * gain).astype(BF)

    def mix(vals):
        return jnp.concatenate(
            [dot_nn(probs_ref[h], vals[:, h * hd : (h + 1) * hd]) for h in range(heads)], axis=1
        )

    loads[0].wait()
    act[...] = mix(dot_nt(normed[...], wv[...]).astype(BF)).astype(BF)

    for here in range(S):
        count = T - 1 + N - 1
        for low in (here - 1, here):
            if 0 <= low < S - 1:
                count += T * (N if (fused and low == 0) else 1)

        @pl.when(s == here)
        def _():
            pl.semaphore_wait(barrier, count)

    def remote(src, dst, send, recv, dev):
        return pltpu.make_async_remote_copy(
            src_ref=src, dst_ref=dst, send_sem=send, recv_sem=recv,
            device_id=dev, device_id_type=MESH,
        )

    def at(dd, ss, jj):
        return {"dp": dd, "section": ss, "tensor": jj}

    def copy_act(k, owner):
        return remote(act, actall.at[owner], act_send.at[k], act_recv.at[k], at(peer(d, k, N), s, i))

    def copy_a(j, owner):
        return remote(partb.at[rows_at(j)], in_a.at[owner], a_send.at[j], a_recv.at[owner], at(d, s + 1, j))

    def copy_tn(k, owner):
        return remote(
            tn.at[rows_at(owner)], tn.at[rows_at(owner)], tn_send.at[k], tn_recv.at[k], at(d, s, peer(i, k, T))
        )

    def copy_d(k):
        j = peer(i, k, T)
        return remote(partb.at[rows_at(j)], in_d.at[k - 1], d_send.at[k], d_recv.at[k], at(d, s, j))

    def copy_s(k, owner):
        return remote(
            gfull.at[rows_at(owner)], gfull.at[rows_at(owner)], s_send.at[k], s_recv.at[k],
            at(d, s, peer(i, k, T)),
        )

    def copy_f(k):
        j = peer(i, k, T)
        return remote(gpartb.at[rows_at(j)], in_f.at[k - 1], f_send.at[k], f_recv.at[k], at(d, s, j))

    def copy_h(j, owner):
        return remote(grow, gfull.at[rows_at(owner)], h_send.at[0, j], h_recv.at[0, owner], at(d, s - 1, j))

    def copy_hd(k, j, owner):
        dd = peer(d, k, N)
        return remote(
            grow.at[:, feats_at(dd)], gall.at[lax.rem(d, N), rows_at(owner)],
            h_send.at[k, j], h_recv.at[k, owner], at(dd, s - 1, j),
        )

    def land_hd(k, owner):
        src = peer(d, N - k, N)
        return remote(
            grow.at[:, feats_at(d)], gall.at[src, rows_at(owner)],
            h_send.at[k, owner], h_recv.at[k, owner], at(d, s, i),
        )

    def copy_x(k):
        dd = peer(d, k, N)
        return remote(gfull.at[:, feats_at(dd)], gall.at[d], x_send.at[k], x_recv.at[k], at(dd, s, i))

    def land_x(k):
        src = peer(d, N - k, N)
        return remote(gfull.at[:, feats_at(d)], gall.at[src], x_send.at[k], x_recv.at[k], at(d, s, i))

    if fused:
        for k in range(1, N):
            copy_act(k, d).start()
        actall[d] = act[...]

    xrows = x_ref[rows_at(i)].astype(F32)
    rrows = lax.rsqrt(jnp.mean(xrows * xrows, axis=-1, keepdims=True) + 1e-06)

    loads[1].wait()
    for c in chunks:
        base = dot_nt(act[...], wd[c, :])
        part[:, c] = base

    loads[2].wait()
    loads[3].wait()

    @pl.when(s == 0)
    def _():
        partb[...] = part[...].astype(BF)

    @pl.when(s > 0)
    def _():
        total = None
        for j in range(T):
            remote(partb.at[rows_at(j)], in_a.at[j], a_send.at[j], a_recv.at[j], at(d, s, i)).wait_recv()
        for j in range(T):
            piece = in_a[j].astype(F32)
            total = piece if total is None else total + piece
        tfloat = total.astype(BF).astype(F32)
        trow[...] = tfloat
        tn[rows_at(i)] = (
            gain * (rrows * tfloat - rrows**3 * xrows * jnp.mean(xrows * tfloat, axis=-1, keepdims=True))
        ).astype(BF)
        for k in range(1, T):
            copy_tn(k, i).start()
        for k in range(1, T):
            copy_tn(k, peer(i, T - k, T)).wait_recv()
        tmix = mix(dot_nt(tn[...], wv[...]).astype(BF)).astype(BF)
        for c in chunks:
            part[:, c] = part[:, c] + dot_nt(tmix, wo[c, :])
        part[rows_at(i)] = part[rows_at(i)] + trow[...]
        partb[...] = part[...].astype(BF)
        for k in range(1, T):
            copy_tn(k, i).wait_send()

    if S > 1:

        @pl.when(s < S - 1)
        def _():
            for j in range(T):
                copy_a(j, i).start()

    @pl.when(s == S - 1)
    def _():
        for k in range(1, T):
            copy_d(k).start()
        total = part[rows_at(i)]
        for k in range(1, T):
            copy_d(k).wait_recv()
        for k in range(1, T):
            total = total + in_d[k - 1].astype(F32)
        tlast = total.astype(BF).astype(F32)
        gfull[rows_at(i)] = (curv[rows_at(i)].astype(F32) * tlast).astype(BF)
        for k in range(1, T):
            copy_s(k, i).start()
        for k in range(1, T):
            copy_s(k, peer(i, T - k, T)).wait_recv()
        for k in range(1, T):
            copy_s(k, i).wait_send()
            copy_d(k).wait_send()

    if S > 1:

        @pl.when(s < S - 1)
        def _():
            for j in range(T):
                copy_a(j, i).wait_send()

        def gather_rows():
            for j in range(T):
                remote(grow, gfull.at[rows_at(j)], h_send.at[0, j], h_recv.at[0, j], at(d, s, i)).wait_recv()

        if fused:
            if S > 2:

                @pl.when(jnp.logical_and(s > 0, s < S - 1))
                def _():
                    gather_rows()

            @pl.when(s == 0)
            def _():
                for k in range(N):
                    for j in range(T):
                        land_hd(k, j).wait_recv()
        else:

            @pl.when(s < S - 1)
            def _():
                gather_rows()

        @pl.when(s > 0)
        def _():
            gm = dot_nn(gfull[...], wo[...]).astype(BF)
            gv = jnp.concatenate(
                [dot_tn(probs_ref[h], gm[:, h * hd : (h + 1) * hd]) for h in range(heads)], axis=1
            ).astype(BF)
            for c in chunks:
                gc = dot_nn(gv, wv[:, c])
                part[:, c] = gc
                gpartb[:, c] = gc.astype(BF)
            for k in range(1, T):
                copy_f(k).start()
            total = part[rows_at(i)]
            for k in range(1, T):
                copy_f(k).wait_recv()
            for k in range(1, T):
                total = total + in_f[k - 1].astype(F32)
            scaled = gain * total
            gx = rrows * scaled - rrows**3 * xrows * jnp.mean(xrows * scaled, axis=-1, keepdims=True)
            grow[...] = (gfull[rows_at(i)].astype(F32) + gx).astype(BF)

            def plain():
                for j in range(T):
                    copy_h(j, i).start()
                for j in range(T):
                    copy_h(j, i).wait_send()

            if fused:

                @pl.when(s == 1)
                def _():
                    for k in range(N):
                        for j in range(T):
                            copy_hd(k, j, i).start()
                    for k in range(N):
                        for j in range(T):
                            copy_hd(k, j, i).wait_send()

                if S > 2:
                    pl.when(s > 1)(plain)
            else:
                plain()
            for k in range(1, T):
                copy_f(k).wait_send()

    if fused:

        def spread():
            for k in range(1, N):
                copy_x(k).start()
            gall[d] = gfull[:, feats_at(d)]
            for k in range(1, N):
                land_x(k).wait_recv()
            for k in range(1, N):
                copy_x(k).wait_send()

        if S > 1:
            pl.when(s > 0)(spread)
        else:
            spread()
        for k in range(1, N):
            copy_act(k, peer(d, N - k, N)).wait_recv()
        prod_ref[...] = dot_tn(
            gall[...].reshape(N * tok, feats), actall[...].reshape(N * tok, act.shape[1])
        )
        for k in range(1, N):
            copy_act(k, d).wait_send()
    else:
        gout_ref[...] = gfull[...]
        actout_ref[...] = act[...]


def per_device(section_input, norm_gain, value_weight, attn_probs, out_weight, direction, curvature):
    x = section_input[0]
    w_val = value_weight[0]
    w_out = out_weight[0]
    w_dir = direction[0]
    probs = attn_probs[0]
    S = lax.axis_size("section")
    T = lax.axis_size("tensor")
    N = lax.axis_size("dp")
    tok, width = x.shape
    hf = w_val.shape[0]
    rows = tok // T
    feats = width // N
    fused = feats % 128 == 0 and feats * N == width
    vm = functools.partial(pl.BlockSpec, memory_space=pltpu.VMEM)
    hbm = functools.partial(pl.BlockSpec, memory_space=pl.ANY)
    if fused:
        outs = jax.ShapeDtypeStruct((feats, hf), F32)
        out_specs = vm()
    else:
        outs = (jax.ShapeDtypeStruct((tok, width), BF), jax.ShapeDtypeStruct((tok, hf), BF))
        out_specs = (vm(), vm())
    sem = pltpu.SemaphoreType.DMA
    wide = N if fused else 1
    scratch = [
        pltpu.VMEM((hf, width), BF),
        pltpu.VMEM((width, hf), BF),
        pltpu.VMEM((width, hf), BF),
        pltpu.VMEM((tok, width), BF),
        pltpu.VMEM((tok, hf), BF),
        pltpu.VMEM((tok, width), F32),
        pltpu.VMEM((tok, width), BF),
        pltpu.VMEM((T, rows, width), BF),
        pltpu.VMEM((T, rows, width), BF),
        pltpu.VMEM((T, rows, width), BF),
        pltpu.VMEM((tok, width), BF),
        pltpu.VMEM((tok, width), BF),
        pltpu.VMEM((tok, width), BF),
        pltpu.VMEM((tok, width), BF),
        pltpu.VMEM((rows, width), F32),
        pltpu.VMEM((rows, width), BF),
        pltpu.VMEM((wide, tok, hf), BF),
        pltpu.VMEM((wide, tok, feats if fused else 128), BF),
        sem((4,)),
        sem((N,)), sem((N,)),
        sem((T,)), sem((T,)),
        sem((T,)), sem((T,)),
        sem((T,)), sem((T,)),
        sem((T,)), sem((T,)),
        sem((T,)), sem((T,)),
        sem((wide, T)), sem((wide, T)),
        sem((N,)), sem((N,)),
    ]
    result = pl.pallas_call(
        functools.partial(kernel, fused, S, T, N),
        out_shape=outs,
        in_specs=[vm(), vm(), vm(), hbm(), hbm(), hbm(), hbm()],
        out_specs=out_specs,
        scratch_shapes=scratch,
        compiler_params=pltpu.CompilerParams(
            collective_id=0, has_side_effects=True, vmem_limit_bytes=56 * 1024 * 1024
        ),
    )(x, norm_gain, probs, w_val, w_dir, w_out, curvature)
    if fused:
        return result[None]
    adjoint, act = result
    product = lax.psum_scatter(
        dot_tn(adjoint, act).astype(BF), "dp", scatter_dimension=0, tiled=True
    ).astype(F32)
    return product[None]


def solution(mesh):
    in_specs = (
        P("section", "dp", None),
        P("section", None),
        P("section", "tensor", None),
        P("section", "tensor", "dp", None),
        P("section", None, "tensor"),
        P("section", None, "tensor"),
        P("dp", None),
    )
    out_specs = P("section", "dp", "tensor")
    return jax.shard_map(
        per_device, mesh=mesh, in_specs=in_specs, out_specs=out_specs, check_vma=False
    )
```

```python
import functools

import jax
import jax.numpy as jnp
from jax import lax
from jax.experimental import pallas as pl
from jax.experimental.pallas import tpu as pltpu
from jax.sharding import PartitionSpec as P

MESH = pl.DeviceIdType.MESH
BF = jnp.bfloat16
F32 = jnp.float32


def dot_nt(a, b):
    return lax.dot_general(a, b, (((1,), (1,)), ((), ())), preferred_element_type=F32)


def dot_tn(a, b):
    return lax.dot_general(a, b, (((0,), (0,)), ((), ())), preferred_element_type=F32)


def dot_nn(a, b):
    return lax.dot_general(a, b, (((1,), (0,)), ((), ())), preferred_element_type=F32)


def kernel(
    fused, S, T, N,
    x_ref, gain_ref, probs_ref, wv_hbm, wd_hbm, wo_hbm, curv_hbm,
    *rest,
):
    if fused:
        prod_ref, rest = rest[0], rest[1:]
    else:
        gout_ref, actout_ref, rest = rest[0], rest[1], rest[2:]
    (
        wv, wd, wo, curv, act, part, partb, in_a, in_d, in_f, gpartb, normed, tn, gfull, trow, grow,
        actall, gall,
        load_sem, act_send, act_recv, a_send, a_recv, tn_send, tn_recv, d_send, d_recv,
        s_send, s_recv, f_send, f_recv, h_send, h_recv, x_send, x_recv,
    ) = rest
    d = lax.axis_index("dp")
    s = lax.axis_index("section")
    i = lax.axis_index("tensor")
    tok, width = x_ref.shape
    rows = tok // T
    heads = probs_ref.shape[0]
    hd = wv.shape[0] // heads
    feats = width // N
    CH = 512 if width % 512 == 0 else width
    chunks = [slice(c, c + CH) for c in range(0, width, CH)]

    def rows_at(j):
        return pl.ds(pl.multiple_of(j * rows, rows), rows)

    def feats_at(j):
        return pl.ds(pl.multiple_of(j * feats, 128), feats)

    def peer(me, k, n):
        return lax.rem(me + k, n)

    loads = [
        pltpu.make_async_copy(src, dst, load_sem.at[k])
        for k, (src, dst) in enumerate(((wv_hbm, wv), (wd_hbm, wd), (wo_hbm, wo), (curv_hbm, curv)))
    ]
    for copy in loads:
        copy.start()

    barrier = pltpu.get_barrier_semaphore()

    def greet(dev):
        pl.semaphore_signal(barrier, inc=1, device_id=dev, device_id_type=MESH)

    for k in range(1, T):
        greet({"dp": d, "section": s, "tensor": peer(i, k, T)})
    for k in range(1, N):
        greet({"dp": peer(d, k, N), "section": s, "tensor": i})
    for low in range(S - 1):
        wide = N if (fused and low == 0) else 1

        @pl.when(s == low)
        def _():
            for k in range(wide):
                for j in range(T):
                    greet({"dp": peer(d, k, N), "section": s + 1, "tensor": j})

        @pl.when(s == low + 1)
        def _():
            for k in range(wide):
                for j in range(T):
                    greet({"dp": peer(d, k, N), "section": s - 1, "tensor": j})

    gain = gain_ref[...]
    xf = x_ref[...].astype(F32)
    rnorm = lax.rsqrt(jnp.mean(xf * xf, axis=-1, keepdims=True) + 1e-06)
    normed[...] = (xf * rnorm * gain).astype(BF)

    def mix(vals):
        return jnp.concatenate(
            [dot_nn(probs_ref[h], vals[:, h * hd : (h + 1) * hd]) for h in range(heads)], axis=1
        )

    loads[0].wait()
    act[...] = mix(dot_nt(normed[...], wv[...]).astype(BF)).astype(BF)

    for here in range(S):
        count = T - 1 + N - 1
        for low in (here - 1, here):
            if 0 <= low < S - 1:
                count += T * (N if (fused and low == 0) else 1)

        @pl.when(s == here)
        def _():
            pl.semaphore_wait(barrier, count)

    def remote(src, dst, send, recv, dev):
        return pltpu.make_async_remote_copy(
            src_ref=src, dst_ref=dst, send_sem=send, recv_sem=recv,
            device_id=dev, device_id_type=MESH,
        )

    def at(dd, ss, jj):
        return {"dp": dd, "section": ss, "tensor": jj}

    def copy_act(k, owner):
        return remote(act, actall.at[owner], act_send.at[k], act_recv.at[k], at(peer(d, k, N), s, i))

    def copy_a(j, owner):
        return remote(partb.at[rows_at(j)], in_a.at[owner], a_send.at[j], a_recv.at[owner], at(d, s + 1, j))

    def copy_tn(k, owner):
        return remote(
            tn.at[rows_at(owner)], tn.at[rows_at(owner)], tn_send.at[k], tn_recv.at[k], at(d, s, peer(i, k, T))
        )

    def copy_d(k):
        j = peer(i, k, T)
        return remote(partb.at[rows_at(j)], in_d.at[k - 1], d_send.at[k], d_recv.at[k], at(d, s, j))

    def copy_s(k, owner):
        return remote(
            gfull.at[rows_at(owner)], gfull.at[rows_at(owner)], s_send.at[k], s_recv.at[k],
            at(d, s, peer(i, k, T)),
        )

    def copy_f(k):
        j = peer(i, k, T)
        return remote(gpartb.at[rows_at(j)], in_f.at[k - 1], f_send.at[k], f_recv.at[k], at(d, s, j))

    def copy_h(j, owner):
        return remote(grow, gfull.at[rows_at(owner)], h_send.at[0, j], h_recv.at[0, owner], at(d, s - 1, j))

    def copy_hd(k, j, owner):
        dd = peer(d, k, N)
        return remote(
            grow.at[:, feats_at(dd)], gall.at[lax.rem(d, N), rows_at(owner)],
            h_send.at[k, j], h_recv.at[k, owner], at(dd, s - 1, j),
        )

    def land_hd(k, owner):
        src = peer(d, N - k, N)
        return remote(
            grow.at[:, feats_at(d)], gall.at[src, rows_at(owner)],
            h_send.at[k, owner], h_recv.at[k, owner], at(d, s, i),
        )

    def copy_x(k):
        dd = peer(d, k, N)
        return remote(gfull.at[:, feats_at(dd)], gall.at[d], x_send.at[k], x_recv.at[k], at(dd, s, i))

    def land_x(k):
        src = peer(d, N - k, N)
        return remote(gfull.at[:, feats_at(d)], gall.at[src], x_send.at[k], x_recv.at[k], at(d, s, i))

    if fused:
        for k in range(1, N):
            copy_act(k, d).start()
        actall[d] = act[...]

    xrows = x_ref[rows_at(i)].astype(F32)
    rrows = lax.rsqrt(jnp.mean(xrows * xrows, axis=-1, keepdims=True) + 1e-06)

    loads[1].wait()
    for c in chunks:
        base = dot_nt(act[...], wd[c, :])
        part[:, c] = base

    loads[2].wait()
    loads[3].wait()

    @pl.when(s == 0)
    def _():
        partb[...] = part[...].astype(BF)

    @pl.when(s > 0)
    def _():
        total = None
        for j in range(T):
            remote(partb.at[rows_at(j)], in_a.at[j], a_send.at[j], a_recv.at[j], at(d, s, i)).wait_recv()
        for j in range(T):
            piece = in_a[j].astype(F32)
            total = piece if total is None else total + piece
        tfloat = total.astype(BF).astype(F32)
        trow[...] = tfloat
        tn[rows_at(i)] = (
            gain * (rrows * tfloat - rrows**3 * xrows * jnp.mean(xrows * tfloat, axis=-1, keepdims=True))
        ).astype(BF)
        for k in range(1, T):
            copy_tn(k, i).start()
        for k in range(1, T):
            copy_tn(k, peer(i, T - k, T)).wait_recv()
        tmix = mix(dot_nt(tn[...], wv[...]).astype(BF)).astype(BF)
        for c in chunks:
            part[:, c] = part[:, c] + dot_nt(tmix, wo[c, :])
        part[rows_at(i)] = part[rows_at(i)] + trow[...]
        partb[...] = part[...].astype(BF)
        for k in range(1, T):
            copy_tn(k, i).wait_send()

    if S > 1:

        @pl.when(s < S - 1)
        def _():
            for j in range(T):
                copy_a(j, i).start()

    @pl.when(s == S - 1)
    def _():
        for k in range(1, T):
            copy_d(k).start()
        total = part[rows_at(i)]
        for k in range(1, T):
            copy_d(k).wait_recv()
        for k in range(1, T):
            total = total + in_d[k - 1].astype(F32)
        tlast = total.astype(BF).astype(F32)
        gfull[rows_at(i)] = (curv[rows_at(i)].astype(F32) * tlast).astype(BF)
        for k in range(1, T):
            copy_s(k, i).start()
        for k in range(1, T):
            copy_s(k, peer(i, T - k, T)).wait_recv()
        for k in range(1, T):
            copy_s(k, i).wait_send()
            copy_d(k).wait_send()

    if S > 1:

        @pl.when(s < S - 1)
        def _():
            for j in range(T):
                copy_a(j, i).wait_send()

        def gather_rows():
            for j in range(T):
                remote(grow, gfull.at[rows_at(j)], h_send.at[0, j], h_recv.at[0, j], at(d, s, i)).wait_recv()

        if fused:
            if S > 2:

                @pl.when(jnp.logical_and(s > 0, s < S - 1))
                def _():
                    gather_rows()

            @pl.when(s == 0)
            def _():
                for k in range(N):
                    for j in range(T):
                        land_hd(k, j).wait_recv()
        else:

            @pl.when(s < S - 1)
            def _():
                gather_rows()

        @pl.when(s > 0)
        def _():
            gm = dot_nn(gfull[...], wo[...]).astype(BF)
            gv = jnp.concatenate(
                [dot_tn(probs_ref[h], gm[:, h * hd : (h + 1) * hd]) for h in range(heads)], axis=1
            ).astype(BF)
            for c in chunks:
                gc = dot_nn(gv, wv[:, c])
                part[:, c] = gc
                gpartb[:, c] = gc.astype(BF)
            for k in range(1, T):
                copy_f(k).start()
            total = part[rows_at(i)]
            for k in range(1, T):
                copy_f(k).wait_recv()
            for k in range(1, T):
                total = total + in_f[k - 1].astype(F32)
            scaled = gain * total
            gx = rrows * scaled - rrows**3 * xrows * jnp.mean(xrows * scaled, axis=-1, keepdims=True)
            grow[...] = (gfull[rows_at(i)].astype(F32) + gx).astype(BF)

            def plain():
                for j in range(T):
                    copy_h(j, i).start()
                for j in range(T):
                    copy_h(j, i).wait_send()

            if fused:

                @pl.when(s == 1)
                def _():
                    for k in range(N):
                        for j in range(T):
                            copy_hd(k, j, i).start()
                    for k in range(N):
                        for j in range(T):
                            copy_hd(k, j, i).wait_send()

                if S > 2:
                    pl.when(s > 1)(plain)
            else:
                plain()
            for k in range(1, T):
                copy_f(k).wait_send()

    if fused:

        def spread():
            for k in range(1, N):
                copy_x(k).start()
            gall[d] = gfull[:, feats_at(d)]
            for k in range(1, N):
                land_x(k).wait_recv()
            for k in range(1, N):
                copy_x(k).wait_send()

        if S > 1:
            pl.when(s > 0)(spread)
        else:
            spread()
        for k in range(1, N):
            copy_act(k, peer(d, N - k, N)).wait_recv()
        prod_ref[...] = dot_tn(
            gall[...].reshape(N * tok, feats), actall[...].reshape(N * tok, act.shape[1])
        )
        for k in range(1, N):
            copy_act(k, d).wait_send()
    else:
        gout_ref[...] = gfull[...]
        actout_ref[...] = act[...]


def kernel_pair(
    T, N,
    x_ref, gain_ref, probs_ref, wv_hbm, wd_hbm, wo_hbm, curv_hbm,
    prod_ref,
    wv, wd, wo, curv, act, part, partb, in_a, in_d, in_f, gpartb, normed, tn, gfull, trow, xrow, grow,
    gain1, actall, gall,
    load_sem, act_send, act_recv, g_send, g_recv, a_send, a_recv, c_send, c_recv, d_send, d_recv,
    e_send, e_recv, f_send, f_recv, h_send, h_recv, x_send, x_recv,
):
    d = lax.axis_index("dp")
    s = lax.axis_index("section")
    i = lax.axis_index("tensor")
    tok, width = x_ref.shape
    rows = tok // T
    half = rows // 2
    heads = probs_ref.shape[0]
    hd = wv.shape[0] // heads
    feats = width // N
    CH = 512 if width % 512 == 0 else width
    chunks = [slice(c, c + CH) for c in range(0, width, CH)]

    def own(ss, jj):
        return pl.ds(pl.multiple_of(jj * rows + (1 - ss) * half, half), half)

    def feats_at(j):
        return pl.ds(pl.multiple_of(j * feats, 128), feats)

    def peer(me, k, n):
        return lax.rem(me + k, n)

    def at(dd, ss, jj):
        return {"dp": dd, "section": ss, "tensor": jj}

    def remote(src, dst, send, recv, dev):
        return pltpu.make_async_remote_copy(
            src_ref=src, dst_ref=dst, send_sem=send, recv_sem=recv,
            device_id=dev, device_id_type=MESH,
        )

    loads = [
        pltpu.make_async_copy(src, dst, load_sem.at[k])
        for k, (src, dst) in enumerate(((wv_hbm, wv), (wd_hbm, wd), (wo_hbm, wo), (curv_hbm, curv)))
    ]
    for copy in loads:
        copy.start()

    barrier = pltpu.get_barrier_semaphore()
    for a in range(N):
        for b in range(2):
            for c in range(T):
                if a or b or c:
                    pl.semaphore_signal(
                        barrier, inc=1, device_id=at(peer(d, a, N), peer(s, b, 2), peer(i, c, T)),
                        device_id_type=MESH,
                    )

    def mix(vals):
        return jnp.concatenate(
            [dot_nn(probs_ref[h], vals[:, h * hd : (h + 1) * hd]) for h in range(heads)], axis=1
        )

    gain = gain_ref[...]
    xf = x_ref[...].astype(F32)
    rnorm = lax.rsqrt(jnp.mean(xf * xf, axis=-1, keepdims=True) + 1e-06)
    normed[...] = (xf * rnorm * gain).astype(BF)
    loads[0].wait()
    act[...] = mix(dot_nt(normed[...], wv[...]).astype(BF)).astype(BF)
    pl.semaphore_wait(barrier, N * 2 * T - 1)

    def copy_act(k, owner):
        return remote(act, actall.at[owner], act_send.at[k], act_recv.at[k], at(peer(d, k, N), s, i))

    lend = (
        remote(x_ref.at[own(0, i)], xrow, g_send.at[0], g_recv.at[0], at(d, 0, i)),
        remote(gain_ref, gain1, g_send.at[1], g_recv.at[1], at(d, 0, i)),
    )

    loads[1].wait()

    def exchange(source, landing, send, recv, home, run):
        for ss in (1 - home, home):
            for k in range(T):
                if ss == home and k == 0:
                    continue
                j = peer(i, k, T)
                run(remote(source.at[own(ss, j)], landing.at[k], send.at[ss, k], recv.at[k], at(d, ss, j)))

    def collect(source, landing, send, recv, home, local):
        first = 1 if local is not None else 0
        for k in range(first, T):
            remote(source.at[own(s, i)], landing.at[k], send.at[0, k], recv.at[k], at(d, s, i)).wait_recv()
        total = local
        for k in range(first, T):
            piece = landing[k].astype(F32)
            total = piece if total is None else total + piece
        return total

    def spread_rows(buf, send, recv, me, run):
        for k in range(T):
            if me == 1 and k == 0:
                continue
            run(remote(buf.at[own(me, i)], buf.at[own(me, i)], send.at[k], recv.at[me, k], at(d, 1, peer(i, k, T))))

    def gather_rows(buf, send, recv):
        for ss in (1, 0):
            for k in range(T):
                if ss == 1 and k == 0:
                    continue
                src = own(ss, peer(i, T - k, T))
                remote(buf.at[src], buf.at[src], send.at[k], recv.at[ss, k], at(d, s, i)).wait_recv()

    def start(copy):
        copy.start()

    def ended(copy):
        copy.wait_send()

    def tangent_rows(total, xr, gn):
        tb = total.astype(BF).astype(F32)
        rr = lax.rsqrt(jnp.mean(xr * xr, axis=-1, keepdims=True) + 1e-06)
        trow[...] = tb
        tn[own(s, i)] = (
            gn * (rr * tb - rr**3 * xr * jnp.mean(xr * tb, axis=-1, keepdims=True))
        ).astype(BF)

    def seed_rows(total):
        tb = (total + trow[...]).astype(BF).astype(F32)
        gfull[own(s, i)] = (curv[own(s, i)].astype(F32) * tb).astype(BF)

    def adjoint_rows(total, xr, gn):
        rr = lax.rsqrt(jnp.mean(xr * xr, axis=-1, keepdims=True) + 1e-06)
        scaled = gn * total
        gx = rr * scaled - rr**3 * xr * jnp.mean(xr * scaled, axis=-1, keepdims=True)
        grow[...] = (gfull[own(s, i)].astype(F32) + gx).astype(BF)

    def hand_over(me, run):
        for k in range(N):
            for j in range(T):
                if me == 0 and k == 0 and j == 0:
                    continue
                dd = peer(d, k, N)
                run(remote(
                    grow.at[:, feats_at(dd)], gall.at[d, own(me, i)],
                    h_send.at[k, j], h_recv.at[me, k, j], at(dd, 0, peer(i, j, T)),
                ))

    @pl.when(s == 0)
    def _():
        for c in chunks:
            base = dot_nt(act[...], wd[c, :])
            part[:, c] = base
            partb[:, c] = base.astype(BF)
        exchange(partb, in_a, a_send, a_recv, 0, start)
        for k in range(1, N):
            copy_act(k, d).start()
        actall[d] = act[...]
        for copy in lend:
            copy.wait_recv()
        xr = xrow[...].astype(F32)
        gn = gain1[...]
        tangent_rows(collect(partb, in_a, a_send, a_recv, 0, part[own(0, i)]), xr, gn)
        spread_rows(tn, c_send, c_recv, 0, start)
        loads[2].wait()
        loads[3].wait()
        seed_rows(collect(partb, in_d, d_send, d_recv, 1, None))
        spread_rows(gfull, e_send, e_recv, 0, start)
        adjoint_rows(collect(gpartb, in_f, f_send, f_recv, 1, None), xr, gn)
        hand_over(0, start)
        gall[d, own(0, i)] = grow[:, feats_at(d)]
        for k in range(1, N):
            copy_act(k, peer(d, N - k, N)).wait_recv()
        for ss in (0, 1):
            for k in range(N):
                for j in range(T):
                    if ss == 0 and k == 0 and j == 0:
                        continue
                    remote(
                        grow.at[:, feats_at(d)],
                        gall.at[peer(d, N - k, N), own(ss, peer(i, T - j, T))],
                        h_send.at[k, j], h_recv.at[ss, k, j], at(d, s, i),
                    ).wait_recv()
        exchange(partb, in_a, a_send, a_recv, 0, ended)
        spread_rows(tn, c_send, c_recv, 0, ended)
        spread_rows(gfull, e_send, e_recv, 0, ended)
        hand_over(0, ended)

    @pl.when(s == 1)
    def _():
        for copy in lend:
            copy.start()
        for k in range(1, N):
            copy_act(k, d).start()
        actall[d] = act[...]
        for c in chunks:
            part[:, c] = dot_nt(act[...], wd[c, :])
        loads[2].wait()
        loads[3].wait()
        xr = x_ref[own(1, i)].astype(F32)
        tangent_rows(collect(partb, in_a, a_send, a_recv, 0, None), xr, gain)
        spread_rows(tn, c_send, c_recv, 1, start)
        gather_rows(tn, c_send, c_recv)
        tmix = mix(dot_nt(tn[...], wv[...]).astype(BF)).astype(BF)
        for c in chunks:
            more = part[:, c] + dot_nt(tmix, wo[c, :])
            part[:, c] = more
            partb[:, c] = more.astype(BF)
        exchange(partb, in_d, d_send, d_recv, 1, start)
        seed_rows(collect(partb, in_d, d_send, d_recv, 1, part[own(1, i)]))
        spread_rows(gfull, e_send, e_recv, 1, start)
        gather_rows(gfull, e_send, e_recv)
        gm = dot_nn(gfull[...], wo[...]).astype(BF)
        gv = jnp.concatenate(
            [dot_tn(probs_ref[h], gm[:, h * hd : (h + 1) * hd]) for h in range(heads)], axis=1
        ).astype(BF)
        for c in chunks:
            gc = dot_nn(gv, wv[:, c])
            part[:, c] = gc
            gpartb[:, c] = gc.astype(BF)
        exchange(gpartb, in_f, f_send, f_recv, 1, start)

        def copy_x(k):
            dd = peer(d, k, N)
            return remote(gfull.at[:, feats_at(dd)], gall.at[d], x_send.at[k], x_recv.at[k], at(dd, s, i))

        for k in range(1, N):
            copy_x(k).start()
        adjoint_rows(collect(gpartb, in_f, f_send, f_recv, 1, part[own(1, i)]), xr, gain)
        hand_over(1, start)
        gall[d] = gfull[:, feats_at(d)]
        for k in range(1, N):
            copy_act(k, peer(d, N - k, N)).wait_recv()
        for k in range(1, N):
            src = peer(d, N - k, N)
            remote(gfull.at[:, feats_at(d)], gall.at[src], x_send.at[k], x_recv.at[k], at(d, s, i)).wait_recv()
        for copy in lend:
            copy.wait_send()
        for k in range(1, N):
            copy_x(k).wait_send()
        spread_rows(tn, c_send, c_recv, 1, ended)
        exchange(partb, in_d, d_send, d_recv, 1, ended)
        spread_rows(gfull, e_send, e_recv, 1, ended)
        exchange(gpartb, in_f, f_send, f_recv, 1, ended)
        hand_over(1, ended)

    prod_ref[...] = dot_tn(
        gall[...].reshape(N * tok, feats), actall[...].reshape(N * tok, act.shape[1])
    )
    for k in range(1, N):
        copy_act(k, d).wait_send()


def call_pair(T, N, x, norm_gain, probs, w_val, w_dir, w_out, curvature):
    tok, width = x.shape
    hf = w_val.shape[0]
    half = tok // T // 2
    feats = width // N
    vm = functools.partial(pl.BlockSpec, memory_space=pltpu.VMEM)
    hbm = functools.partial(pl.BlockSpec, memory_space=pl.ANY)
    sem = pltpu.SemaphoreType.DMA
    scratch = [
        pltpu.VMEM((hf, width), BF),
        pltpu.VMEM((width, hf), BF),
        pltpu.VMEM((width, hf), BF),
        pltpu.VMEM((tok, width), BF),
        pltpu.VMEM((tok, hf), BF),
        pltpu.VMEM((tok, width), F32),
        pltpu.VMEM((tok, width), BF),
        pltpu.VMEM((T, half, width), BF),
        pltpu.VMEM((T, half, width), BF),
        pltpu.VMEM((T, half, width), BF),
        pltpu.VMEM((tok, width), BF),
        pltpu.VMEM((tok, width), BF),
        pltpu.VMEM((tok, width), BF),
        pltpu.VMEM((tok, width), BF),
        pltpu.VMEM((half, width), F32),
        pltpu.VMEM((half, width), BF),
        pltpu.VMEM((half, width), BF),
        pltpu.VMEM((1, width), F32),
        pltpu.VMEM((N, tok, hf), BF),
        pltpu.VMEM((N, tok, feats), BF),
        sem((4,)),
        sem((N,)), sem((N,)),
        sem((2,)), sem((2,)),
        sem((2, T)), sem((T,)),
        sem((T,)), sem((2, T)),
        sem((2, T)), sem((T,)),
        sem((T,)), sem((2, T)),
        sem((2, T)), sem((T,)),
        sem((N, T)), sem((2, N, T)),
        sem((N,)), sem((N,)),
    ]
    return pl.pallas_call(
        functools.partial(kernel_pair, T, N),
        out_shape=jax.ShapeDtypeStruct((feats, hf), F32),
        in_specs=[vm(), vm(), vm(), hbm(), hbm(), hbm(), hbm()],
        out_specs=vm(),
        scratch_shapes=scratch,
        compiler_params=pltpu.CompilerParams(
            collective_id=0, has_side_effects=True, vmem_limit_bytes=56 * 1024 * 1024
        ),
    )(x, norm_gain, probs, w_val, w_dir, w_out, curvature)


def per_device(section_input, norm_gain, value_weight, attn_probs, out_weight, direction, curvature):
    x = section_input[0]
    w_val = value_weight[0]
    w_out = out_weight[0]
    w_dir = direction[0]
    probs = attn_probs[0]
    S = lax.axis_size("section")
    T = lax.axis_size("tensor")
    N = lax.axis_size("dp")
    tok, width = x.shape
    hf = w_val.shape[0]
    rows = tok // T
    feats = width // N
    fused = feats % 128 == 0 and feats * N == width
    if fused and S == 2 and rows % 32 == 0:
        return call_pair(T, N, x, norm_gain, probs, w_val, w_dir, w_out, curvature)[None]
    vm = functools.partial(pl.BlockSpec, memory_space=pltpu.VMEM)
    hbm = functools.partial(pl.BlockSpec, memory_space=pl.ANY)
    if fused:
        outs = jax.ShapeDtypeStruct((feats, hf), F32)
        out_specs = vm()
    else:
        outs = (jax.ShapeDtypeStruct((tok, width), BF), jax.ShapeDtypeStruct((tok, hf), BF))
        out_specs = (vm(), vm())
    sem = pltpu.SemaphoreType.DMA
    wide = N if fused else 1
    scratch = [
        pltpu.VMEM((hf, width), BF),
        pltpu.VMEM((width, hf), BF),
        pltpu.VMEM((width, hf), BF),
        pltpu.VMEM((tok, width), BF),
        pltpu.VMEM((tok, hf), BF),
        pltpu.VMEM((tok, width), F32),
        pltpu.VMEM((tok, width), BF),
        pltpu.VMEM((T, rows, width), BF),
        pltpu.VMEM((T, rows, width), BF),
        pltpu.VMEM((T, rows, width), BF),
        pltpu.VMEM((tok, width), BF),
        pltpu.VMEM((tok, width), BF),
        pltpu.VMEM((tok, width), BF),
        pltpu.VMEM((tok, width), BF),
        pltpu.VMEM((rows, width), F32),
        pltpu.VMEM((rows, width), BF),
        pltpu.VMEM((wide, tok, hf), BF),
        pltpu.VMEM((wide, tok, feats if fused else 128), BF),
        sem((4,)),
        sem((N,)), sem((N,)),
        sem((T,)), sem((T,)),
        sem((T,)), sem((T,)),
        sem((T,)), sem((T,)),
        sem((T,)), sem((T,)),
        sem((T,)), sem((T,)),
        sem((wide, T)), sem((wide, T)),
        sem((N,)), sem((N,)),
    ]
    result = pl.pallas_call(
        functools.partial(kernel, fused, S, T, N),
        out_shape=outs,
        in_specs=[vm(), vm(), vm(), hbm(), hbm(), hbm(), hbm()],
        out_specs=out_specs,
        scratch_shapes=scratch,
        compiler_params=pltpu.CompilerParams(
            collective_id=0, has_side_effects=True, vmem_limit_bytes=56 * 1024 * 1024
        ),
    )(x, norm_gain, probs, w_val, w_dir, w_out, curvature)
    if fused:
        return result[None]
    adjoint, act = result
    product = lax.psum_scatter(
        dot_tn(adjoint, act).astype(BF), "dp", scatter_dimension=0, tiled=True
    ).astype(F32)
    return product[None]


def solution(mesh):
    in_specs = (
        P("section", "dp", None),
        P("section", None),
        P("section", "tensor", None),
        P("section", "tensor", "dp", None),
        P("section", None, "tensor"),
        P("section", None, "tensor"),
        P("dp", None),
    )
    out_specs = P("section", "dp", "tensor")
    return jax.shard_map(
        per_device, mesh=mesh, in_specs=in_specs, out_specs=out_specs, check_vma=False
    )
```

```python
import functools

import jax
import jax.numpy as jnp
from jax import lax
from jax.experimental import pallas as pl
from jax.experimental.pallas import tpu as pltpu
from jax.sharding import PartitionSpec as P

MESH = pl.DeviceIdType.MESH
BF = jnp.bfloat16
F32 = jnp.float32


def dot_nt(a, b):
    return lax.dot_general(a, b, (((1,), (1,)), ((), ())), preferred_element_type=F32)


def dot_tn(a, b):
    return lax.dot_general(a, b, (((0,), (0,)), ((), ())), preferred_element_type=F32)


def dot_nn(a, b):
    return lax.dot_general(a, b, (((1,), (0,)), ((), ())), preferred_element_type=F32)


def kernel(
    fused, S, T, N,
    x_ref, gain_ref, probs_ref, wv_hbm, wd_hbm, wo_hbm, curv_hbm,
    *rest,
):
    if fused:
        prod_ref, rest = rest[0], rest[1:]
    else:
        gout_ref, actout_ref, rest = rest[0], rest[1], rest[2:]
    (
        wv, wd, wo, curv, act, part, partb, in_a, in_d, in_f, gpartb, normed, tn, gfull, trow, grow,
        actall, gall,
        load_sem, act_send, act_recv, a_send, a_recv, tn_send, tn_recv, d_send, d_recv,
        s_send, s_recv, f_send, f_recv, h_send, h_recv, x_send, x_recv,
    ) = rest
    d = lax.axis_index("dp")
    s = lax.axis_index("section")
    i = lax.axis_index("tensor")
    tok, width = x_ref.shape
    rows = tok // T
    heads = probs_ref.shape[0]
    hd = wv.shape[0] // heads
    feats = width // N
    CH = 512 if width % 512 == 0 else width
    chunks = [slice(c, c + CH) for c in range(0, width, CH)]

    def rows_at(j):
        return pl.ds(pl.multiple_of(j * rows, rows), rows)

    def feats_at(j):
        return pl.ds(pl.multiple_of(j * feats, 128), feats)

    def peer(me, k, n):
        return lax.rem(me + k, n)

    loads = [
        pltpu.make_async_copy(src, dst, load_sem.at[k])
        for k, (src, dst) in enumerate(((wv_hbm, wv), (wd_hbm, wd), (wo_hbm, wo), (curv_hbm, curv)))
    ]
    for copy in loads:
        copy.start()

    barrier = pltpu.get_barrier_semaphore()

    def greet(dev):
        pl.semaphore_signal(barrier, inc=1, device_id=dev, device_id_type=MESH)

    for k in range(1, T):
        greet({"dp": d, "section": s, "tensor": peer(i, k, T)})
    for k in range(1, N):
        greet({"dp": peer(d, k, N), "section": s, "tensor": i})
    for low in range(S - 1):
        wide = N if (fused and low == 0) else 1

        @pl.when(s == low)
        def _():
            for k in range(wide):
                for j in range(T):
                    greet({"dp": peer(d, k, N), "section": s + 1, "tensor": j})

        @pl.when(s == low + 1)
        def _():
            for k in range(wide):
                for j in range(T):
                    greet({"dp": peer(d, k, N), "section": s - 1, "tensor": j})

    gain = gain_ref[...]
    xf = x_ref[...].astype(F32)
    rnorm = lax.rsqrt(jnp.mean(xf * xf, axis=-1, keepdims=True) + 1e-06)
    normed[...] = (xf * rnorm * gain).astype(BF)

    def mix(vals):
        return jnp.concatenate(
            [dot_nn(probs_ref[h], vals[:, h * hd : (h + 1) * hd]) for h in range(heads)], axis=1
        )

    loads[0].wait()
    act[...] = mix(dot_nt(normed[...], wv[...]).astype(BF)).astype(BF)

    for here in range(S):
        count = T - 1 + N - 1
        for low in (here - 1, here):
            if 0 <= low < S - 1:
                count += T * (N if (fused and low == 0) else 1)

        @pl.when(s == here)
        def _():
            pl.semaphore_wait(barrier, count)

    def remote(src, dst, send, recv, dev):
        return pltpu.make_async_remote_copy(
            src_ref=src, dst_ref=dst, send_sem=send, recv_sem=recv,
            device_id=dev, device_id_type=MESH,
        )

    def at(dd, ss, jj):
        return {"dp": dd, "section": ss, "tensor": jj}

    def copy_act(k, owner):
        return remote(act, actall.at[owner], act_send.at[k], act_recv.at[k], at(peer(d, k, N), s, i))

    def copy_a(j, owner):
        return remote(partb.at[rows_at(j)], in_a.at[owner], a_send.at[j], a_recv.at[owner], at(d, s + 1, j))

    def copy_tn(k, owner):
        return remote(
            tn.at[rows_at(owner)], tn.at[rows_at(owner)], tn_send.at[k], tn_recv.at[k], at(d, s, peer(i, k, T))
        )

    def copy_d(k):
        j = peer(i, k, T)
        return remote(partb.at[rows_at(j)], in_d.at[k - 1], d_send.at[k], d_recv.at[k], at(d, s, j))

    def copy_s(k, owner):
        return remote(
            gfull.at[rows_at(owner)], gfull.at[rows_at(owner)], s_send.at[k], s_recv.at[k],
            at(d, s, peer(i, k, T)),
        )

    def copy_f(k):
        j = peer(i, k, T)
        return remote(gpartb.at[rows_at(j)], in_f.at[k - 1], f_send.at[k], f_recv.at[k], at(d, s, j))

    def copy_h(j, owner):
        return remote(grow, gfull.at[rows_at(owner)], h_send.at[0, j], h_recv.at[0, owner], at(d, s - 1, j))

    def copy_hd(k, j, owner):
        dd = peer(d, k, N)
        return remote(
            grow.at[:, feats_at(dd)], gall.at[lax.rem(d, N), rows_at(owner)],
            h_send.at[k, j], h_recv.at[k, owner], at(dd, s - 1, j),
        )

    def land_hd(k, owner):
        src = peer(d, N - k, N)
        return remote(
            grow.at[:, feats_at(d)], gall.at[src, rows_at(owner)],
            h_send.at[k, owner], h_recv.at[k, owner], at(d, s, i),
        )

    def copy_x(k):
        dd = peer(d, k, N)
        return remote(gfull.at[:, feats_at(dd)], gall.at[d], x_send.at[k], x_recv.at[k], at(dd, s, i))

    def land_x(k):
        src = peer(d, N - k, N)
        return remote(gfull.at[:, feats_at(d)], gall.at[src], x_send.at[k], x_recv.at[k], at(d, s, i))

    if fused:
        for k in range(1, N):
            copy_act(k, d).start()
        actall[d] = act[...]

    xrows = x_ref[rows_at(i)].astype(F32)
    rrows = lax.rsqrt(jnp.mean(xrows * xrows, axis=-1, keepdims=True) + 1e-06)

    loads[1].wait()
    for c in chunks:
        base = dot_nt(act[...], wd[c, :])
        part[:, c] = base

    loads[2].wait()
    loads[3].wait()

    @pl.when(s == 0)
    def _():
        partb[...] = part[...].astype(BF)

    @pl.when(s > 0)
    def _():
        total = None
        for j in range(T):
            remote(partb.at[rows_at(j)], in_a.at[j], a_send.at[j], a_recv.at[j], at(d, s, i)).wait_recv()
        for j in range(T):
            piece = in_a[j].astype(F32)
            total = piece if total is None else total + piece
        tfloat = total.astype(BF).astype(F32)
        trow[...] = tfloat
        tn[rows_at(i)] = (
            gain * (rrows * tfloat - rrows**3 * xrows * jnp.mean(xrows * tfloat, axis=-1, keepdims=True))
        ).astype(BF)
        for k in range(1, T):
            copy_tn(k, i).start()
        for k in range(1, T):
            copy_tn(k, peer(i, T - k, T)).wait_recv()
        tmix = mix(dot_nt(tn[...], wv[...]).astype(BF)).astype(BF)
        for c in chunks:
            part[:, c] = part[:, c] + dot_nt(tmix, wo[c, :])
        part[rows_at(i)] = part[rows_at(i)] + trow[...]
        partb[...] = part[...].astype(BF)
        for k in range(1, T):
            copy_tn(k, i).wait_send()

    if S > 1:

        @pl.when(s < S - 1)
        def _():
            for j in range(T):
                copy_a(j, i).start()

    @pl.when(s == S - 1)
    def _():
        for k in range(1, T):
            copy_d(k).start()
        total = part[rows_at(i)]
        for k in range(1, T):
            copy_d(k).wait_recv()
        for k in range(1, T):
            total = total + in_d[k - 1].astype(F32)
        tlast = total.astype(BF).astype(F32)
        gfull[rows_at(i)] = (curv[rows_at(i)].astype(F32) * tlast).astype(BF)
        for k in range(1, T):
            copy_s(k, i).start()
        for k in range(1, T):
            copy_s(k, peer(i, T - k, T)).wait_recv()
        for k in range(1, T):
            copy_s(k, i).wait_send()
            copy_d(k).wait_send()

    if S > 1:

        @pl.when(s < S - 1)
        def _():
            for j in range(T):
                copy_a(j, i).wait_send()

        def gather_rows():
            for j in range(T):
                remote(grow, gfull.at[rows_at(j)], h_send.at[0, j], h_recv.at[0, j], at(d, s, i)).wait_recv()

        if fused:
            if S > 2:

                @pl.when(jnp.logical_and(s > 0, s < S - 1))
                def _():
                    gather_rows()

            @pl.when(s == 0)
            def _():
                for k in range(N):
                    for j in range(T):
                        land_hd(k, j).wait_recv()
        else:

            @pl.when(s < S - 1)
            def _():
                gather_rows()

        @pl.when(s > 0)
        def _():
            gm = dot_nn(gfull[...], wo[...]).astype(BF)
            gv = jnp.concatenate(
                [dot_tn(probs_ref[h], gm[:, h * hd : (h + 1) * hd]) for h in range(heads)], axis=1
            ).astype(BF)
            for c in chunks:
                gc = dot_nn(gv, wv[:, c])
                part[:, c] = gc
                gpartb[:, c] = gc.astype(BF)
            for k in range(1, T):
                copy_f(k).start()
            total = part[rows_at(i)]
            for k in range(1, T):
                copy_f(k).wait_recv()
            for k in range(1, T):
                total = total + in_f[k - 1].astype(F32)
            scaled = gain * total
            gx = rrows * scaled - rrows**3 * xrows * jnp.mean(xrows * scaled, axis=-1, keepdims=True)
            grow[...] = (gfull[rows_at(i)].astype(F32) + gx).astype(BF)

            def plain():
                for j in range(T):
                    copy_h(j, i).start()
                for j in range(T):
                    copy_h(j, i).wait_send()

            if fused:

                @pl.when(s == 1)
                def _():
                    for k in range(N):
                        for j in range(T):
                            copy_hd(k, j, i).start()
                    for k in range(N):
                        for j in range(T):
                            copy_hd(k, j, i).wait_send()

                if S > 2:
                    pl.when(s > 1)(plain)
            else:
                plain()
            for k in range(1, T):
                copy_f(k).wait_send()

    if fused:

        def spread():
            for k in range(1, N):
                copy_x(k).start()
            gall[d] = gfull[:, feats_at(d)]
            for k in range(1, N):
                land_x(k).wait_recv()
            for k in range(1, N):
                copy_x(k).wait_send()

        if S > 1:
            pl.when(s > 0)(spread)
        else:
            spread()
        for k in range(1, N):
            copy_act(k, peer(d, N - k, N)).wait_recv()
        prod_ref[...] = dot_tn(
            gall[...].reshape(N * tok, feats), actall[...].reshape(N * tok, act.shape[1])
        )
        for k in range(1, N):
            copy_act(k, d).wait_send()
    else:
        gout_ref[...] = gfull[...]
        actout_ref[...] = act[...]


def kernel_pair(
    T, N,
    x_ref, gain_ref, probs_ref, wv_hbm, wd_hbm, wo_hbm, curv_hbm,
    prod_ref,
    wv, wd, wo, curv, act, part, partb, in_a, in_d, in_f, gpartb, normed, tn, gfull, trow, xrow, grow,
    gain1, actall, gall, stage,
    load_sem, act_send, act_recv, g_send, g_recv, a_send, a_recv, c_send, c_recv, c_relay, d_send, d_recv,
    e_send, e_recv, e_relay, f_send, f_recv, h_send, h_recv, r_send, r_recv, x_send, x_recv,
):
    d = lax.axis_index("dp")
    s = lax.axis_index("section")
    i = lax.axis_index("tensor")
    tok, width = x_ref.shape
    rows = tok // T
    half = rows // 2
    heads = probs_ref.shape[0]
    hd = wv.shape[0] // heads
    feats = width // N
    Q = 2
    wide = width // Q
    CH = 512 if wide % 512 == 0 else wide
    cols = [slice(q * wide, (q + 1) * wide) for q in range(Q)]
    parts = [[slice(c, c + CH) for c in range(q * wide, (q + 1) * wide, CH)] for q in range(Q)]
    order = [k for k in range(1, T) if k in (1, T - 1)] + [k for k in range(2, T - 1)]

    def own(ss, jj):
        return pl.ds(pl.multiple_of(jj * rows + (1 - ss) * half, half), half)

    def feats_at(j):
        return pl.ds(pl.multiple_of(j * feats, 128), feats)

    def peer(me, k, n):
        return lax.rem(me + k, n)

    def at(dd, ss, jj):
        return {"dp": dd, "section": ss, "tensor": jj}

    def remote(src, dst, send, recv, dev):
        return pltpu.make_async_remote_copy(
            src_ref=src, dst_ref=dst, send_sem=send, recv_sem=recv,
            device_id=dev, device_id_type=MESH,
        )

    loads = [
        pltpu.make_async_copy(src, dst, load_sem.at[k])
        for k, (src, dst) in enumerate(((wv_hbm, wv), (wd_hbm, wd), (wo_hbm, wo), (curv_hbm, curv)))
    ]
    for copy in loads:
        copy.start()

    barrier = pltpu.get_barrier_semaphore()
    for a in range(N):
        for b in range(2):
            for c in range(T):
                if a or b or c:
                    pl.semaphore_signal(
                        barrier, inc=1, device_id=at(peer(d, a, N), peer(s, b, 2), peer(i, c, T)),
                        device_id_type=MESH,
                    )

    def mix(vals):
        return jnp.concatenate(
            [dot_nn(probs_ref[h], vals[:, h * hd : (h + 1) * hd]) for h in range(heads)], axis=1
        )

    gain = gain_ref[...]
    xf = x_ref[...].astype(F32)
    rnorm = lax.rsqrt(jnp.mean(xf * xf, axis=-1, keepdims=True) + 1e-06)
    normed[...] = (xf * rnorm * gain).astype(BF)
    loads[0].wait()
    act[...] = mix(dot_nt(normed[...], wv[...]).astype(BF)).astype(BF)
    pl.semaphore_wait(barrier, N * 2 * T - 1)

    def copy_act(k, owner):
        return remote(act, actall.at[owner], act_send.at[k], act_recv.at[k], at(peer(d, k, N), s, i))

    lend = (
        remote(x_ref.at[own(0, i)], xrow, g_send.at[0], g_recv.at[0], at(d, 0, i)),
        remote(gain_ref, gain1, g_send.at[1], g_recv.at[1], at(d, 0, i)),
    )

    loads[1].wait()

    def exchange(q, source, landing, send, recv, home, run):
        c = cols[q]
        for ss in (1 - home, home):
            for k in range(T):
                if ss == home and k == 0:
                    continue
                j = peer(i, k, T)
                run(remote(
                    source.at[own(ss, j), c], landing.at[k, :, c], send.at[q, ss, k], recv.at[q, k], at(d, ss, j)
                ))

    def collect(q, source, landing, send, recv, local):
        c = cols[q]
        first = 1 if local is not None else 0
        for k in range(first, T):
            remote(
                source.at[own(s, i), c], landing.at[k, :, c], send.at[q, 0, k], recv.at[q, k], at(d, s, i)
            ).wait_recv()
        total = local
        for k in range(first, T):
            piece = landing[k, :, c].astype(F32)
            total = piece if total is None else total + piece
        return total

    def spread_rows(q, buf, send, recv, relay, me, run):
        r = own(me, i)
        src = buf.at[r, cols[q]]
        if me == 0:
            run(remote(src, src, send.at[q, 0, 0], recv.at[q, 0, 0], at(d, 1, i)))
        for k in range(1, T):
            land = recv.at[q, 1, k] if me == 1 else relay.at[q, k]
            run(remote(src, src, send.at[q, 0, k], land, at(d, me, peer(i, k, T))))

    def pass_on(q, buf, send, recv, relay, run, wait):
        for k in order:
            src = buf.at[own(0, peer(i, T - k, T)), cols[q]]
            if wait:
                remote(src, src, send.at[q, 0, k], relay.at[q, k], at(d, s, i)).wait_recv()
            run(remote(src, src, send.at[q, 1, k], recv.at[q, 0, k], at(d, 1, i)))

    def gather_rows(q, buf, send, recv):
        for ss in (1, 0):
            for k in range(T):
                if ss == 1 and k == 0:
                    continue
                src = buf.at[own(ss, peer(i, T - k, T)), cols[q]]
                remote(src, src, send.at[q, 0, k], recv.at[q, ss, k], at(d, s, i)).wait_recv()

    def start(copy):
        copy.start()

    def ended(copy):
        copy.wait_send()

    def tangent_rows(total, xr, gn):
        tb = total.astype(BF).astype(F32)
        rr = lax.rsqrt(jnp.mean(xr * xr, axis=-1, keepdims=True) + 1e-06)
        trow[...] = tb
        tn[own(s, i)] = (
            gn * (rr * tb - rr**3 * xr * jnp.mean(xr * tb, axis=-1, keepdims=True))
        ).astype(BF)

    def seed_rows(q, total):
        c = cols[q]
        tb = (total + trow[:, c]).astype(BF).astype(F32)
        gfull[own(s, i), c] = (curv[own(s, i), c].astype(F32) * tb).astype(BF)

    def adjoint_rows(total, xr, gn):
        rr = lax.rsqrt(jnp.mean(xr * xr, axis=-1, keepdims=True) + 1e-06)
        scaled = gn * total
        gx = rr * scaled - rr**3 * xr * jnp.mean(xr * scaled, axis=-1, keepdims=True)
        grow[...] = (gfull[own(s, i)].astype(F32) + gx).astype(BF)

    def hand_over(me, run):
        for j in [0] + order if me == 1 else order + [0]:
            for k in range(N):
                if me == 0 and k == 0 and j == 0:
                    continue
                dd = peer(d, k, N)
                src = grow.at[:, feats_at(dd)]
                if me == 1 and j > 0:
                    run(remote(src, stage.at[k, j], h_send.at[k, j], r_recv.at[k, j], at(dd, 1, peer(i, j, T))))
                else:
                    run(remote(
                        src, gall.at[d, own(me, i)], h_send.at[k, j], h_recv.at[me, k, j], at(dd, 0, peer(i, j, T))
                    ))

    def hand_on(run, wait):
        for j in order:
            for k in range(N):
                if wait:
                    remote(
                        grow.at[:, feats_at(d)], stage.at[k, j], h_send.at[k, j], r_recv.at[k, j], at(d, s, i)
                    ).wait_recv()
                run(remote(
                    stage.at[k, j], gall.at[peer(d, N - k, N), own(1, peer(i, T - j, T))],
                    r_send.at[k, j], h_recv.at[1, k, j], at(d, 0, i),
                ))

    def whole(sums):
        return jnp.concatenate(sums, axis=1)

    @pl.when(s == 0)
    def _():
        for q in range(Q):
            for c in parts[q]:
                base = dot_nt(act[...], wd[c, :])
                part[:, c] = base
                partb[:, c] = base.astype(BF)
            exchange(q, partb, in_a, a_send, a_recv, 0, start)
        for k in range(1, N):
            copy_act(k, d).start()
        actall[d] = act[...]
        for copy in lend:
            copy.wait_recv()
        xr = xrow[...].astype(F32)
        gn = gain1[...]
        tangent_rows(
            whole([collect(q, partb, in_a, a_send, a_recv, part[own(0, i), cols[q]]) for q in range(Q)]), xr, gn
        )
        for q in range(Q):
            spread_rows(q, tn, c_send, c_recv, c_relay, 0, start)
        for q in range(Q):
            pass_on(q, tn, c_send, c_recv, c_relay, start, True)
        loads[2].wait()
        loads[3].wait()
        for q in range(Q):
            seed_rows(q, collect(q, partb, in_d, d_send, d_recv, None))
            spread_rows(q, gfull, e_send, e_recv, e_relay, 0, start)
        for q in range(Q):
            pass_on(q, gfull, e_send, e_recv, e_relay, start, True)
        adjoint_rows(whole([collect(q, gpartb, in_f, f_send, f_recv, None) for q in range(Q)]), xr, gn)
        hand_over(0, start)
        gall[d, own(0, i)] = grow[:, feats_at(d)]
        for k in range(1, N):
            copy_act(k, peer(d, N - k, N)).wait_recv()
        for ss in (0, 1):
            for k in range(N):
                for j in range(T):
                    if ss == 0 and k == 0 and j == 0:
                        continue
                    remote(
                        grow.at[:, feats_at(d)],
                        gall.at[peer(d, N - k, N), own(ss, peer(i, T - j, T))],
                        h_send.at[k, j], h_recv.at[ss, k, j], at(d, s, i),
                    ).wait_recv()
        for q in range(Q):
            exchange(q, partb, in_a, a_send, a_recv, 0, ended)
            spread_rows(q, tn, c_send, c_recv, c_relay, 0, ended)
            pass_on(q, tn, c_send, c_recv, c_relay, ended, False)
            spread_rows(q, gfull, e_send, e_recv, e_relay, 0, ended)
            pass_on(q, gfull, e_send, e_recv, e_relay, ended, False)
        hand_over(0, ended)

    @pl.when(s == 1)
    def _():
        for copy in lend:
            copy.start()
        for k in range(1, N):
            copy_act(k, d).start()
        actall[d] = act[...]
        for q in range(Q):
            for c in parts[q]:
                part[:, c] = dot_nt(act[...], wd[c, :])
        loads[2].wait()
        loads[3].wait()
        xr = x_ref[own(1, i)].astype(F32)
        tangent_rows(whole([collect(q, partb, in_a, a_send, a_recv, None) for q in range(Q)]), xr, gain)
        for q in range(Q):
            spread_rows(q, tn, c_send, c_recv, None, 1, start)
        tv = None
        for q in range(Q):
            gather_rows(q, tn, c_send, c_recv)
            more = dot_nt(tn[:, cols[q]], wv[:, cols[q]])
            tv = more if tv is None else tv + more
        tmix = mix(tv.astype(BF)).astype(BF)
        for q in range(Q):
            for c in parts[q]:
                more = part[:, c] + dot_nt(tmix, wo[c, :])
                part[:, c] = more
                partb[:, c] = more.astype(BF)
            exchange(q, partb, in_d, d_send, d_recv, 1, start)
        for q in range(Q):
            seed_rows(q, collect(q, partb, in_d, d_send, d_recv, part[own(1, i), cols[q]]))
            spread_rows(q, gfull, e_send, e_recv, None, 1, start)
        gm = None
        for q in range(Q):
            gather_rows(q, gfull, e_send, e_recv)
            more = dot_nn(gfull[:, cols[q]], wo[cols[q], :])
            gm = more if gm is None else gm + more
        gm = gm.astype(BF)
        gv = jnp.concatenate(
            [dot_tn(probs_ref[h], gm[:, h * hd : (h + 1) * hd]) for h in range(heads)], axis=1
        ).astype(BF)
        for q in range(Q):
            for c in parts[q]:
                gc = dot_nn(gv, wv[:, c])
                part[:, c] = gc
                gpartb[:, c] = gc.astype(BF)
            exchange(q, gpartb, in_f, f_send, f_recv, 1, start)

        def copy_x(k):
            dd = peer(d, k, N)
            return remote(gfull.at[:, feats_at(dd)], gall.at[d], x_send.at[k], x_recv.at[k], at(dd, s, i))

        for k in range(1, N):
            copy_x(k).start()
        adjoint_rows(
            whole([collect(q, gpartb, in_f, f_send, f_recv, part[own(1, i), cols[q]]) for q in range(Q)]), xr, gain
        )
        hand_over(1, start)
        hand_on(start, True)
        gall[d] = gfull[:, feats_at(d)]
        for k in range(1, N):
            copy_act(k, peer(d, N - k, N)).wait_recv()
        for k in range(1, N):
            src = peer(d, N - k, N)
            remote(gfull.at[:, feats_at(d)], gall.at[src], x_send.at[k], x_recv.at[k], at(d, s, i)).wait_recv()
        for copy in lend:
            copy.wait_send()
        for k in range(1, N):
            copy_x(k).wait_send()
        for q in range(Q):
            spread_rows(q, tn, c_send, c_recv, None, 1, ended)
            exchange(q, partb, in_d, d_send, d_recv, 1, ended)
            spread_rows(q, gfull, e_send, e_recv, None, 1, ended)
            exchange(q, gpartb, in_f, f_send, f_recv, 1, ended)
        hand_over(1, ended)
        hand_on(ended, False)

    prod_ref[...] = dot_tn(
        gall[...].reshape(N * tok, feats), actall[...].reshape(N * tok, act.shape[1])
    )
    for k in range(1, N):
        copy_act(k, d).wait_send()


def call_pair(T, N, x, norm_gain, probs, w_val, w_dir, w_out, curvature):
    tok, width = x.shape
    hf = w_val.shape[0]
    half = tok // T // 2
    feats = width // N
    vm = functools.partial(pl.BlockSpec, memory_space=pltpu.VMEM)
    hbm = functools.partial(pl.BlockSpec, memory_space=pl.ANY)
    sem = pltpu.SemaphoreType.DMA
    scratch = [
        pltpu.VMEM((hf, width), BF),
        pltpu.VMEM((width, hf), BF),
        pltpu.VMEM((width, hf), BF),
        pltpu.VMEM((tok, width), BF),
        pltpu.VMEM((tok, hf), BF),
        pltpu.VMEM((tok, width), F32),
        pltpu.VMEM((tok, width), BF),
        pltpu.VMEM((T, half, width), BF),
        pltpu.VMEM((T, half, width), BF),
        pltpu.VMEM((T, half, width), BF),
        pltpu.VMEM((tok, width), BF),
        pltpu.VMEM((tok, width), BF),
        pltpu.VMEM((tok, width), BF),
        pltpu.VMEM((tok, width), BF),
        pltpu.VMEM((half, width), F32),
        pltpu.VMEM((half, width), BF),
        pltpu.VMEM((half, width), BF),
        pltpu.VMEM((1, width), F32),
        pltpu.VMEM((N, tok, hf), BF),
        pltpu.VMEM((N, tok, feats), BF),
        pltpu.VMEM((N, T, half, feats), BF),
        sem((4,)),
        sem((N,)), sem((N,)),
        sem((2,)), sem((2,)),
        sem((2, 2, T)), sem((2, T)),
        sem((2, 2, T)), sem((2, 2, T)), sem((2, T)),
        sem((2, 2, T)), sem((2, T)),
        sem((2, 2, T)), sem((2, 2, T)), sem((2, T)),
        sem((2, 2, T)), sem((2, T)),
        sem((N, T)), sem((2, N, T)), sem((N, T)), sem((N, T)),
        sem((N,)), sem((N,)),
    ]
    return pl.pallas_call(
        functools.partial(kernel_pair, T, N),
        out_shape=jax.ShapeDtypeStruct((feats, hf), F32),
        in_specs=[vm(), vm(), vm(), hbm(), hbm(), hbm(), hbm()],
        out_specs=vm(),
        scratch_shapes=scratch,
        compiler_params=pltpu.CompilerParams(
            collective_id=0, has_side_effects=True, vmem_limit_bytes=56 * 1024 * 1024
        ),
    )(x, norm_gain, probs, w_val, w_dir, w_out, curvature)


def per_device(section_input, norm_gain, value_weight, attn_probs, out_weight, direction, curvature):
    x = section_input[0]
    w_val = value_weight[0]
    w_out = out_weight[0]
    w_dir = direction[0]
    probs = attn_probs[0]
    S = lax.axis_size("section")
    T = lax.axis_size("tensor")
    N = lax.axis_size("dp")
    tok, width = x.shape
    hf = w_val.shape[0]
    rows = tok // T
    feats = width // N
    fused = feats % 128 == 0 and feats * N == width
    if fused and S == 2 and rows % 32 == 0 and width % 256 == 0:
        return call_pair(T, N, x, norm_gain, probs, w_val, w_dir, w_out, curvature)[None]
    vm = functools.partial(pl.BlockSpec, memory_space=pltpu.VMEM)
    hbm = functools.partial(pl.BlockSpec, memory_space=pl.ANY)
    if fused:
        outs = jax.ShapeDtypeStruct((feats, hf), F32)
        out_specs = vm()
    else:
        outs = (jax.ShapeDtypeStruct((tok, width), BF), jax.ShapeDtypeStruct((tok, hf), BF))
        out_specs = (vm(), vm())
    sem = pltpu.SemaphoreType.DMA
    wide = N if fused else 1
    scratch = [
        pltpu.VMEM((hf, width), BF),
        pltpu.VMEM((width, hf), BF),
        pltpu.VMEM((width, hf), BF),
        pltpu.VMEM((tok, width), BF),
        pltpu.VMEM((tok, hf), BF),
        pltpu.VMEM((tok, width), F32),
        pltpu.VMEM((tok, width), BF),
        pltpu.VMEM((T, rows, width), BF),
        pltpu.VMEM((T, rows, width), BF),
        pltpu.VMEM((T, rows, width), BF),
        pltpu.VMEM((tok, width), BF),
        pltpu.VMEM((tok, width), BF),
        pltpu.VMEM((tok, width), BF),
        pltpu.VMEM((tok, width), BF),
        pltpu.VMEM((rows, width), F32),
        pltpu.VMEM((rows, width), BF),
        pltpu.VMEM((wide, tok, hf), BF),
        pltpu.VMEM((wide, tok, feats if fused else 128), BF),
        sem((4,)),
        sem((N,)), sem((N,)),
        sem((T,)), sem((T,)),
        sem((T,)), sem((T,)),
        sem((T,)), sem((T,)),
        sem((T,)), sem((T,)),
        sem((T,)), sem((T,)),
        sem((wide, T)), sem((wide, T)),
        sem((N,)), sem((N,)),
    ]
    result = pl.pallas_call(
        functools.partial(kernel, fused, S, T, N),
        out_shape=outs,
        in_specs=[vm(), vm(), vm(), hbm(), hbm(), hbm(), hbm()],
        out_specs=out_specs,
        scratch_shapes=scratch,
        compiler_params=pltpu.CompilerParams(
            collective_id=0, has_side_effects=True, vmem_limit_bytes=56 * 1024 * 1024
        ),
    )(x, norm_gain, probs, w_val, w_dir, w_out, curvature)
    if fused:
        return result[None]
    adjoint, act = result
    product = lax.psum_scatter(
        dot_tn(adjoint, act).astype(BF), "dp", scatter_dimension=0, tiled=True
    ).astype(F32)
    return product[None]


def solution(mesh):
    in_specs = (
        P("section", "dp", None),
        P("section", None),
        P("section", "tensor", None),
        P("section", "tensor", "dp", None),
        P("section", None, "tensor"),
        P("section", None, "tensor"),
        P("dp", None),
    )
    out_specs = P("section", "dp", "tensor")
    return jax.shard_map(
        per_device, mesh=mesh, in_specs=in_specs, out_specs=out_specs, check_vma=False
    )
```

```python
import functools

import jax
import jax.numpy as jnp
from jax import lax
from jax.experimental import pallas as pl
from jax.experimental.pallas import tpu as pltpu
from jax.sharding import PartitionSpec as P

MESH = pl.DeviceIdType.MESH
BF = jnp.bfloat16
F32 = jnp.float32
HALVES = 2
RELAY_ROWS = False
RELAY_SUMS = True
RELAY_ADJ = False


def dot_nt(a, b):
    return lax.dot_general(a, b, (((1,), (1,)), ((), ())), preferred_element_type=F32)


def dot_tn(a, b):
    return lax.dot_general(a, b, (((0,), (0,)), ((), ())), preferred_element_type=F32)


def dot_nn(a, b):
    return lax.dot_general(a, b, (((1,), (0,)), ((), ())), preferred_element_type=F32)


def kernel(
    fused, S, T, N,
    x_ref, gain_ref, probs_ref, wv_hbm, wd_hbm, wo_hbm, curv_hbm,
    *rest,
):
    if fused:
        prod_ref, rest = rest[0], rest[1:]
    else:
        gout_ref, actout_ref, rest = rest[0], rest[1], rest[2:]
    (
        wv, wd, wo, curv, act, part, partb, in_a, in_d, in_f, gpartb, normed, tn, gfull, trow, grow,
        actall, gall,
        load_sem, act_send, act_recv, a_send, a_recv, tn_send, tn_recv, d_send, d_recv,
        s_send, s_recv, f_send, f_recv, h_send, h_recv, x_send, x_recv,
    ) = rest
    d = lax.axis_index("dp")
    s = lax.axis_index("section")
    i = lax.axis_index("tensor")
    tok, width = x_ref.shape
    rows = tok // T
    heads = probs_ref.shape[0]
    hd = wv.shape[0] // heads
    feats = width // N
    CH = 512 if width % 512 == 0 else width
    chunks = [slice(c, c + CH) for c in range(0, width, CH)]

    def rows_at(j):
        return pl.ds(pl.multiple_of(j * rows, rows), rows)

    def feats_at(j):
        return pl.ds(pl.multiple_of(j * feats, 128), feats)

    def peer(me, k, n):
        return lax.rem(me + k, n)

    loads = [
        pltpu.make_async_copy(src, dst, load_sem.at[k])
        for k, (src, dst) in enumerate(((wv_hbm, wv), (wd_hbm, wd), (wo_hbm, wo), (curv_hbm, curv)))
    ]
    for copy in loads:
        copy.start()

    barrier = pltpu.get_barrier_semaphore()

    def greet(dev):
        pl.semaphore_signal(barrier, inc=1, device_id=dev, device_id_type=MESH)

    for k in range(1, T):
        greet({"dp": d, "section": s, "tensor": peer(i, k, T)})
    for k in range(1, N):
        greet({"dp": peer(d, k, N), "section": s, "tensor": i})
    for low in range(S - 1):
        wide = N if (fused and low == 0) else 1

        @pl.when(s == low)
        def _():
            for k in range(wide):
                for j in range(T):
                    greet({"dp": peer(d, k, N), "section": s + 1, "tensor": j})

        @pl.when(s == low + 1)
        def _():
            for k in range(wide):
                for j in range(T):
                    greet({"dp": peer(d, k, N), "section": s - 1, "tensor": j})

    gain = gain_ref[...]
    xf = x_ref[...].astype(F32)
    rnorm = lax.rsqrt(jnp.mean(xf * xf, axis=-1, keepdims=True) + 1e-06)
    normed[...] = (xf * rnorm * gain).astype(BF)

    def mix(vals):
        return jnp.concatenate(
            [dot_nn(probs_ref[h], vals[:, h * hd : (h + 1) * hd]) for h in range(heads)], axis=1
        )

    loads[0].wait()
    act[...] = mix(dot_nt(normed[...], wv[...]).astype(BF)).astype(BF)

    for here in range(S):
        count = T - 1 + N - 1
        for low in (here - 1, here):
            if 0 <= low < S - 1:
                count += T * (N if (fused and low == 0) else 1)

        @pl.when(s == here)
        def _():
            pl.semaphore_wait(barrier, count)

    def remote(src, dst, send, recv, dev):
        return pltpu.make_async_remote_copy(
            src_ref=src, dst_ref=dst, send_sem=send, recv_sem=recv,
            device_id=dev, device_id_type=MESH,
        )

    def at(dd, ss, jj):
        return {"dp": dd, "section": ss, "tensor": jj}

    def copy_act(k, owner):
        return remote(act, actall.at[owner], act_send.at[k], act_recv.at[k], at(peer(d, k, N), s, i))

    def copy_a(j, owner):
        return remote(partb.at[rows_at(j)], in_a.at[owner], a_send.at[j], a_recv.at[owner], at(d, s + 1, j))

    def copy_tn(k, owner):
        return remote(
            tn.at[rows_at(owner)], tn.at[rows_at(owner)], tn_send.at[k], tn_recv.at[k], at(d, s, peer(i, k, T))
        )

    def copy_d(k):
        j = peer(i, k, T)
        return remote(partb.at[rows_at(j)], in_d.at[k - 1], d_send.at[k], d_recv.at[k], at(d, s, j))

    def copy_s(k, owner):
        return remote(
            gfull.at[rows_at(owner)], gfull.at[rows_at(owner)], s_send.at[k], s_recv.at[k],
            at(d, s, peer(i, k, T)),
        )

    def copy_f(k):
        j = peer(i, k, T)
        return remote(gpartb.at[rows_at(j)], in_f.at[k - 1], f_send.at[k], f_recv.at[k], at(d, s, j))

    def copy_h(j, owner):
        return remote(grow, gfull.at[rows_at(owner)], h_send.at[0, j], h_recv.at[0, owner], at(d, s - 1, j))

    def copy_hd(k, j, owner):
        dd = peer(d, k, N)
        return remote(
            grow.at[:, feats_at(dd)], gall.at[lax.rem(d, N), rows_at(owner)],
            h_send.at[k, j], h_recv.at[k, owner], at(dd, s - 1, j),
        )

    def land_hd(k, owner):
        src = peer(d, N - k, N)
        return remote(
            grow.at[:, feats_at(d)], gall.at[src, rows_at(owner)],
            h_send.at[k, owner], h_recv.at[k, owner], at(d, s, i),
        )

    def copy_x(k):
        dd = peer(d, k, N)
        return remote(gfull.at[:, feats_at(dd)], gall.at[d], x_send.at[k], x_recv.at[k], at(dd, s, i))

    def land_x(k):
        src = peer(d, N - k, N)
        return remote(gfull.at[:, feats_at(d)], gall.at[src], x_send.at[k], x_recv.at[k], at(d, s, i))

    if fused:
        for k in range(1, N):
            copy_act(k, d).start()
        actall[d] = act[...]

    xrows = x_ref[rows_at(i)].astype(F32)
    rrows = lax.rsqrt(jnp.mean(xrows * xrows, axis=-1, keepdims=True) + 1e-06)

    loads[1].wait()
    for c in chunks:
        base = dot_nt(act[...], wd[c, :])
        part[:, c] = base

    loads[2].wait()
    loads[3].wait()

    @pl.when(s == 0)
    def _():
        partb[...] = part[...].astype(BF)

    @pl.when(s > 0)
    def _():
        total = None
        for j in range(T):
            remote(partb.at[rows_at(j)], in_a.at[j], a_send.at[j], a_recv.at[j], at(d, s, i)).wait_recv()
        for j in range(T):
            piece = in_a[j].astype(F32)
            total = piece if total is None else total + piece
        tfloat = total.astype(BF).astype(F32)
        trow[...] = tfloat
        tn[rows_at(i)] = (
            gain * (rrows * tfloat - rrows**3 * xrows * jnp.mean(xrows * tfloat, axis=-1, keepdims=True))
        ).astype(BF)
        for k in range(1, T):
            copy_tn(k, i).start()
        for k in range(1, T):
            copy_tn(k, peer(i, T - k, T)).wait_recv()
        tmix = mix(dot_nt(tn[...], wv[...]).astype(BF)).astype(BF)
        for c in chunks:
            part[:, c] = part[:, c] + dot_nt(tmix, wo[c, :])
        part[rows_at(i)] = part[rows_at(i)] + trow[...]
        partb[...] = part[...].astype(BF)
        for k in range(1, T):
            copy_tn(k, i).wait_send()

    if S > 1:

        @pl.when(s < S - 1)
        def _():
            for j in range(T):
                copy_a(j, i).start()

    @pl.when(s == S - 1)
    def _():
        for k in range(1, T):
            copy_d(k).start()
        total = part[rows_at(i)]
        for k in range(1, T):
            copy_d(k).wait_recv()
        for k in range(1, T):
            total = total + in_d[k - 1].astype(F32)
        tlast = total.astype(BF).astype(F32)
        gfull[rows_at(i)] = (curv[rows_at(i)].astype(F32) * tlast).astype(BF)
        for k in range(1, T):
            copy_s(k, i).start()
        for k in range(1, T):
            copy_s(k, peer(i, T - k, T)).wait_recv()
        for k in range(1, T):
            copy_s(k, i).wait_send()
            copy_d(k).wait_send()

    if S > 1:

        @pl.when(s < S - 1)
        def _():
            for j in range(T):
                copy_a(j, i).wait_send()

        def gather_rows():
            for j in range(T):
                remote(grow, gfull.at[rows_at(j)], h_send.at[0, j], h_recv.at[0, j], at(d, s, i)).wait_recv()

        if fused:
            if S > 2:

                @pl.when(jnp.logical_and(s > 0, s < S - 1))
                def _():
                    gather_rows()

            @pl.when(s == 0)
            def _():
                for k in range(N):
                    for j in range(T):
                        land_hd(k, j).wait_recv()
        else:

            @pl.when(s < S - 1)
            def _():
                gather_rows()

        @pl.when(s > 0)
        def _():
            gm = dot_nn(gfull[...], wo[...]).astype(BF)
            gv = jnp.concatenate(
                [dot_tn(probs_ref[h], gm[:, h * hd : (h + 1) * hd]) for h in range(heads)], axis=1
            ).astype(BF)
            for c in chunks:
                gc = dot_nn(gv, wv[:, c])
                part[:, c] = gc
                gpartb[:, c] = gc.astype(BF)
            for k in range(1, T):
                copy_f(k).start()
            total = part[rows_at(i)]
            for k in range(1, T):
                copy_f(k).wait_recv()
            for k in range(1, T):
                total = total + in_f[k - 1].astype(F32)
            scaled = gain * total
            gx = rrows * scaled - rrows**3 * xrows * jnp.mean(xrows * scaled, axis=-1, keepdims=True)
            grow[...] = (gfull[rows_at(i)].astype(F32) + gx).astype(BF)

            def plain():
                for j in range(T):
                    copy_h(j, i).start()
                for j in range(T):
                    copy_h(j, i).wait_send()

            if fused:

                @pl.when(s == 1)
                def _():
                    for k in range(N):
                        for j in range(T):
                            copy_hd(k, j, i).start()
                    for k in range(N):
                        for j in range(T):
                            copy_hd(k, j, i).wait_send()

                if S > 2:
                    pl.when(s > 1)(plain)
            else:
                plain()
            for k in range(1, T):
                copy_f(k).wait_send()

    if fused:

        def spread():
            for k in range(1, N):
                copy_x(k).start()
            gall[d] = gfull[:, feats_at(d)]
            for k in range(1, N):
                land_x(k).wait_recv()
            for k in range(1, N):
                copy_x(k).wait_send()

        if S > 1:
            pl.when(s > 0)(spread)
        else:
            spread()
        for k in range(1, N):
            copy_act(k, peer(d, N - k, N)).wait_recv()
        prod_ref[...] = dot_tn(
            gall[...].reshape(N * tok, feats), actall[...].reshape(N * tok, act.shape[1])
        )
        for k in range(1, N):
            copy_act(k, d).wait_send()
    else:
        gout_ref[...] = gfull[...]
        actout_ref[...] = act[...]


def kernel_pair(
    T, N,
    x_ref, gain_ref, probs_ref, wv_hbm, wd_hbm, wo_hbm, curv_hbm,
    prod_ref,
    wv, wd, wo, curv, act, part, partb, in_a, in_d, in_f, gpartb, normed, tn, gfull, trow, xrow, grow,
    gain1, actall, gall, stage, hop1_buf, hop2_buf,
    load_sem, act_send, act_recv, g_send, g_recv, a_send, a_recv, c_send, c_recv, c_relay, d_send, d_recv,
    e_send, e_recv, e_relay, f_send, f_recv, h_send, h_recv, r_send, r_recv, x_send, x_recv, hop_send, hop_recv,
):
    hop1 = (hop1_buf, hop_send.at[0], hop_recv.at[0])
    hop2 = (hop2_buf, hop_send.at[1], hop_recv.at[1])
    d = lax.axis_index("dp")
    s = lax.axis_index("section")
    i = lax.axis_index("tensor")
    tok, width = x_ref.shape
    rows = tok // T
    half = rows // 2
    heads = probs_ref.shape[0]
    hd = wv.shape[0] // heads
    feats = width // N
    Q = HALVES
    wide = width // Q
    CH = 512 if wide % 512 == 0 else wide
    cols = [slice(q * wide, (q + 1) * wide) for q in range(Q)]
    parts = [[slice(c, c + CH) for c in range(q * wide, (q + 1) * wide, CH)] for q in range(Q)]
    order = [k for k in range(1, T) if k in (1, T - 1)] + [k for k in range(2, T - 1)]

    def own(ss, jj):
        return pl.ds(pl.multiple_of(jj * rows + (1 - ss) * half, half), half)

    def feats_at(j):
        return pl.ds(pl.multiple_of(j * feats, 128), feats)

    def peer(me, k, n):
        return lax.rem(me + k, n)

    def at(dd, ss, jj):
        return {"dp": dd, "section": ss, "tensor": jj}

    def remote(src, dst, send, recv, dev):
        return pltpu.make_async_remote_copy(
            src_ref=src, dst_ref=dst, send_sem=send, recv_sem=recv,
            device_id=dev, device_id_type=MESH,
        )

    loads = [
        pltpu.make_async_copy(src, dst, load_sem.at[k])
        for k, (src, dst) in enumerate(((wv_hbm, wv), (wd_hbm, wd), (wo_hbm, wo), (curv_hbm, curv)))
    ]
    for copy in loads:
        copy.start()

    barrier = pltpu.get_barrier_semaphore()
    for a in range(N):
        for b in range(2):
            for c in range(T):
                if a or b or c:
                    pl.semaphore_signal(
                        barrier, inc=1, device_id=at(peer(d, a, N), peer(s, b, 2), peer(i, c, T)),
                        device_id_type=MESH,
                    )

    def mix(vals):
        return jnp.concatenate(
            [dot_nn(probs_ref[h], vals[:, h * hd : (h + 1) * hd]) for h in range(heads)], axis=1
        )

    gain = gain_ref[...]
    xf = x_ref[...].astype(F32)
    rnorm = lax.rsqrt(jnp.mean(xf * xf, axis=-1, keepdims=True) + 1e-06)
    normed[...] = (xf * rnorm * gain).astype(BF)
    loads[0].wait()
    act[...] = mix(dot_nt(normed[...], wv[...]).astype(BF)).astype(BF)
    pl.semaphore_wait(barrier, N * 2 * T - 1)

    def copy_act(k, owner):
        return remote(act, actall.at[owner], act_send.at[k], act_recv.at[k], at(peer(d, k, N), s, i))

    lend = (
        remote(x_ref.at[own(0, i)], xrow, g_send.at[0], g_recv.at[0], at(d, 0, i)),
        remote(gain_ref, gain1, g_send.at[1], g_recv.at[1], at(d, 0, i)),
    )

    loads[1].wait()

    def exchange(q, source, landing, send, recv, hop, home, run):
        c = cols[q]
        for ss in (1 - home, home):
            for k in range(T):
                if ss == home and k == 0:
                    continue
                j = peer(i, k, T)
                src = source.at[own(ss, j), c]
                if RELAY_SUMS and ss != home and k > 0:
                    run(remote(src, hop[0].at[k, :, c], send.at[q, ss, k], hop[2].at[q, k], at(d, ss, i)))
                else:
                    run(remote(src, landing.at[k, :, c], send.at[q, ss, k], recv.at[q, k], at(d, ss, j)))

    def forward(q, landing, recv, hop, run, wait):
        c = cols[q]
        for k in order if RELAY_SUMS else []:
            src = hop[0].at[k, :, c]
            if wait:
                remote(src, src, hop[1].at[q, k], hop[2].at[q, k], at(d, s, i)).wait_recv()
            run(remote(src, landing.at[k, :, c], hop[1].at[q, k], recv.at[q, k], at(d, s, peer(i, k, T))))

    def collect(q, source, landing, send, recv, local):
        c = cols[q]
        first = 1 if local is not None else 0
        for k in range(first, T):
            remote(
                source.at[own(s, i), c], landing.at[k, :, c], send.at[q, 0, k], recv.at[q, k], at(d, s, i)
            ).wait_recv()
        total = local
        for k in range(first, T):
            piece = landing[k, :, c].astype(F32)
            total = piece if total is None else total + piece
        return total

    def spread_rows(q, buf, send, recv, relay, me, run):
        r = own(me, i)
        src = buf.at[r, cols[q]]
        if me == 0:
            run(remote(src, src, send.at[q, 0, 0], recv.at[q, 0, 0], at(d, 1, i)))
        for k in range(1, T):
            if me == 1:
                land, where = recv.at[q, 1, k], 1
            elif RELAY_ROWS:
                land, where = relay.at[q, k], 0
            else:
                land, where = recv.at[q, 0, k], 1
            run(remote(src, src, send.at[q, 0, k], land, at(d, where, peer(i, k, T))))

    def pass_on(q, buf, send, recv, relay, run, wait):
        for k in order if RELAY_ROWS else []:
            src = buf.at[own(0, peer(i, T - k, T)), cols[q]]
            if wait:
                remote(src, src, send.at[q, 0, k], relay.at[q, k], at(d, s, i)).wait_recv()
            run(remote(src, src, send.at[q, 1, k], recv.at[q, 0, k], at(d, 1, i)))

    def gather_rows(q, buf, send, recv):
        for ss in (1, 0):
            for k in range(T):
                if ss == 1 and k == 0:
                    continue
                src = buf.at[own(ss, peer(i, T - k, T)), cols[q]]
                remote(src, src, send.at[q, 0, k], recv.at[q, ss, k], at(d, s, i)).wait_recv()

    def start(copy):
        copy.start()

    def ended(copy):
        copy.wait_send()

    def tangent_rows(total, xr, gn):
        tb = total.astype(BF).astype(F32)
        rr = lax.rsqrt(jnp.mean(xr * xr, axis=-1, keepdims=True) + 1e-06)
        trow[...] = tb
        tn[own(s, i)] = (
            gn * (rr * tb - rr**3 * xr * jnp.mean(xr * tb, axis=-1, keepdims=True))
        ).astype(BF)

    def seed_rows(q, total):
        c = cols[q]
        tb = (total + trow[:, c]).astype(BF).astype(F32)
        gfull[own(s, i), c] = (curv[own(s, i), c].astype(F32) * tb).astype(BF)

    def adjoint_rows(total, xr, gn):
        rr = lax.rsqrt(jnp.mean(xr * xr, axis=-1, keepdims=True) + 1e-06)
        scaled = gn * total
        gx = rr * scaled - rr**3 * xr * jnp.mean(xr * scaled, axis=-1, keepdims=True)
        grow[...] = (gfull[own(s, i)].astype(F32) + gx).astype(BF)

    def hand_over(me, run):
        for j in [0] + order if me == 1 else order + [0]:
            for k in range(N):
                if me == 0 and k == 0 and j == 0:
                    continue
                dd = peer(d, k, N)
                src = grow.at[:, feats_at(dd)]
                if RELAY_ADJ and me == 1 and j > 0:
                    run(remote(src, stage.at[k, j], h_send.at[k, j], r_recv.at[k, j], at(dd, 1, peer(i, j, T))))
                else:
                    run(remote(
                        src, gall.at[d, own(me, i)], h_send.at[k, j], h_recv.at[me, k, j], at(dd, 0, peer(i, j, T))
                    ))

    def hand_on(run, wait):
        for j in order if RELAY_ADJ else []:
            for k in range(N):
                if wait:
                    remote(
                        grow.at[:, feats_at(d)], stage.at[k, j], h_send.at[k, j], r_recv.at[k, j], at(d, s, i)
                    ).wait_recv()
                run(remote(
                    stage.at[k, j], gall.at[peer(d, N - k, N), own(1, peer(i, T - j, T))],
                    r_send.at[k, j], h_recv.at[1, k, j], at(d, 0, i),
                ))

    def whole(sums):
        return jnp.concatenate(sums, axis=1)

    @pl.when(s == 0)
    def _():
        for q in range(Q):
            for c in parts[q]:
                base = dot_nt(act[...], wd[c, :])
                part[:, c] = base
                partb[:, c] = base.astype(BF)
            exchange(q, partb, in_a, a_send, a_recv, hop1, 0, start)
        for k in range(1, N):
            copy_act(k, d).start()
        actall[d] = act[...]
        for copy in lend:
            copy.wait_recv()
        xr = xrow[...].astype(F32)
        gn = gain1[...]
        tangent_rows(
            whole([collect(q, partb, in_a, a_send, a_recv, part[own(0, i), cols[q]]) for q in range(Q)]), xr, gn
        )
        for q in range(Q):
            spread_rows(q, tn, c_send, c_recv, c_relay, 0, start)
        for q in range(Q):
            pass_on(q, tn, c_send, c_recv, c_relay, start, True)
        loads[2].wait()
        loads[3].wait()
        for q in range(Q):
            forward(q, in_d, d_recv, hop1, start, True)
        for q in range(Q):
            seed_rows(q, collect(q, partb, in_d, d_send, d_recv, None))
            spread_rows(q, gfull, e_send, e_recv, e_relay, 0, start)
        for q in range(Q):
            pass_on(q, gfull, e_send, e_recv, e_relay, start, True)
        for q in range(Q):
            forward(q, in_f, f_recv, hop2, start, True)
        adjoint_rows(whole([collect(q, gpartb, in_f, f_send, f_recv, None) for q in range(Q)]), xr, gn)
        hand_over(0, start)
        gall[d, own(0, i)] = grow[:, feats_at(d)]
        for k in range(1, N):
            copy_act(k, peer(d, N - k, N)).wait_recv()
        for ss in (0, 1):
            for k in range(N):
                for j in range(T):
                    if ss == 0 and k == 0 and j == 0:
                        continue
                    remote(
                        grow.at[:, feats_at(d)],
                        gall.at[peer(d, N - k, N), own(ss, peer(i, T - j, T))],
                        h_send.at[k, j], h_recv.at[ss, k, j], at(d, s, i),
                    ).wait_recv()
        for q in range(Q):
            exchange(q, partb, in_a, a_send, a_recv, hop1, 0, ended)
            spread_rows(q, tn, c_send, c_recv, c_relay, 0, ended)
            pass_on(q, tn, c_send, c_recv, c_relay, ended, False)
            spread_rows(q, gfull, e_send, e_recv, e_relay, 0, ended)
            pass_on(q, gfull, e_send, e_recv, e_relay, ended, False)
        for q in range(Q):
            forward(q, in_d, d_recv, hop1, ended, False)
            forward(q, in_f, f_recv, hop2, ended, False)
        hand_over(0, ended)

    @pl.when(s == 1)
    def _():
        for copy in lend:
            copy.start()
        for k in range(1, N):
            copy_act(k, d).start()
        actall[d] = act[...]
        for q in range(Q):
            for c in parts[q]:
                part[:, c] = dot_nt(act[...], wd[c, :])
        loads[2].wait()
        loads[3].wait()
        xr = x_ref[own(1, i)].astype(F32)
        for q in range(Q):
            forward(q, in_a, a_recv, hop1, start, True)
        tangent_rows(whole([collect(q, partb, in_a, a_send, a_recv, None) for q in range(Q)]), xr, gain)
        for q in range(Q):
            spread_rows(q, tn, c_send, c_recv, None, 1, start)
        tv = None
        for q in range(Q):
            gather_rows(q, tn, c_send, c_recv)
            more = dot_nt(tn[:, cols[q]], wv[:, cols[q]])
            tv = more if tv is None else tv + more
        tmix = mix(tv.astype(BF)).astype(BF)
        for q in range(Q):
            for c in parts[q]:
                more = part[:, c] + dot_nt(tmix, wo[c, :])
                part[:, c] = more
                partb[:, c] = more.astype(BF)
            exchange(q, partb, in_d, d_send, d_recv, hop1, 1, start)
        for q in range(Q):
            seed_rows(q, collect(q, partb, in_d, d_send, d_recv, part[own(1, i), cols[q]]))
            spread_rows(q, gfull, e_send, e_recv, None, 1, start)
        gm = None
        for q in range(Q):
            gather_rows(q, gfull, e_send, e_recv)
            more = dot_nn(gfull[:, cols[q]], wo[cols[q], :])
            gm = more if gm is None else gm + more
        gm = gm.astype(BF)
        gv = jnp.concatenate(
            [dot_tn(probs_ref[h], gm[:, h * hd : (h + 1) * hd]) for h in range(heads)], axis=1
        ).astype(BF)
        for q in range(Q):
            for c in parts[q]:
                gc = dot_nn(gv, wv[:, c])
                part[:, c] = gc
                gpartb[:, c] = gc.astype(BF)
            exchange(q, gpartb, in_f, f_send, f_recv, hop2, 1, start)

        def copy_x(k):
            dd = peer(d, k, N)
            return remote(gfull.at[:, feats_at(dd)], gall.at[d], x_send.at[k], x_recv.at[k], at(dd, s, i))

        for k in range(1, N):
            copy_x(k).start()
        adjoint_rows(
            whole([collect(q, gpartb, in_f, f_send, f_recv, part[own(1, i), cols[q]]) for q in range(Q)]), xr, gain
        )
        hand_over(1, start)
        hand_on(start, True)
        gall[d] = gfull[:, feats_at(d)]
        for k in range(1, N):
            copy_act(k, peer(d, N - k, N)).wait_recv()
        for k in range(1, N):
            src = peer(d, N - k, N)
            remote(gfull.at[:, feats_at(d)], gall.at[src], x_send.at[k], x_recv.at[k], at(d, s, i)).wait_recv()
        for copy in lend:
            copy.wait_send()
        for k in range(1, N):
            copy_x(k).wait_send()
        for q in range(Q):
            spread_rows(q, tn, c_send, c_recv, None, 1, ended)
            exchange(q, partb, in_d, d_send, d_recv, hop1, 1, ended)
            spread_rows(q, gfull, e_send, e_recv, None, 1, ended)
            exchange(q, gpartb, in_f, f_send, f_recv, hop2, 1, ended)
        for q in range(Q):
            forward(q, in_a, a_recv, hop1, ended, False)
        hand_over(1, ended)
        hand_on(ended, False)

    prod_ref[...] = dot_tn(
        gall[...].reshape(N * tok, feats), actall[...].reshape(N * tok, act.shape[1])
    )
    for k in range(1, N):
        copy_act(k, d).wait_send()


def call_pair(T, N, x, norm_gain, probs, w_val, w_dir, w_out, curvature):
    tok, width = x.shape
    hf = w_val.shape[0]
    half = tok // T // 2
    feats = width // N
    vm = functools.partial(pl.BlockSpec, memory_space=pltpu.VMEM)
    hbm = functools.partial(pl.BlockSpec, memory_space=pl.ANY)
    sem = pltpu.SemaphoreType.DMA
    scratch = [
        pltpu.VMEM((hf, width), BF),
        pltpu.VMEM((width, hf), BF),
        pltpu.VMEM((width, hf), BF),
        pltpu.VMEM((tok, width), BF),
        pltpu.VMEM((tok, hf), BF),
        pltpu.VMEM((tok, width), F32),
        pltpu.VMEM((tok, width), BF),
        pltpu.VMEM((T, half, width), BF),
        pltpu.VMEM((T, half, width), BF),
        pltpu.VMEM((T, half, width), BF),
        pltpu.VMEM((tok, width), BF),
        pltpu.VMEM((tok, width), BF),
        pltpu.VMEM((tok, width), BF),
        pltpu.VMEM((tok, width), BF),
        pltpu.VMEM((half, width), F32),
        pltpu.VMEM((half, width), BF),
        pltpu.VMEM((half, width), BF),
        pltpu.VMEM((1, width), F32),
        pltpu.VMEM((N, tok, hf), BF),
        pltpu.VMEM((N, tok, feats), BF),
        pltpu.VMEM((N, T, half, feats), BF),
        pltpu.VMEM((T, half, width), BF),
        pltpu.VMEM((T, half, width), BF),
        sem((4,)),
        sem((N,)), sem((N,)),
        sem((2,)), sem((2,)),
        sem((2, 2, T)), sem((2, T)),
        sem((2, 2, T)), sem((2, 2, T)), sem((2, T)),
        sem((2, 2, T)), sem((2, T)),
        sem((2, 2, T)), sem((2, 2, T)), sem((2, T)),
        sem((2, 2, T)), sem((2, T)),
        sem((N, T)), sem((2, N, T)), sem((N, T)), sem((N, T)),
        sem((N,)), sem((N,)),
        sem((2, 2, T)), sem((2, 2, T)),
    ]
    return pl.pallas_call(
        functools.partial(kernel_pair, T, N),
        out_shape=jax.ShapeDtypeStruct((feats, hf), F32),
        in_specs=[vm(), vm(), vm(), hbm(), hbm(), hbm(), hbm()],
        out_specs=vm(),
        scratch_shapes=scratch,
        compiler_params=pltpu.CompilerParams(
            collective_id=0, has_side_effects=True, vmem_limit_bytes=56 * 1024 * 1024
        ),
    )(x, norm_gain, probs, w_val, w_dir, w_out, curvature)


def per_device(section_input, norm_gain, value_weight, attn_probs, out_weight, direction, curvature):
    x = section_input[0]
    w_val = value_weight[0]
    w_out = out_weight[0]
    w_dir = direction[0]
    probs = attn_probs[0]
    S = lax.axis_size("section")
    T = lax.axis_size("tensor")
    N = lax.axis_size("dp")
    tok, width = x.shape
    hf = w_val.shape[0]
    rows = tok // T
    feats = width // N
    fused = feats % 128 == 0 and feats * N == width
    if fused and S == 2 and rows % 32 == 0 and width % 256 == 0:
        return call_pair(T, N, x, norm_gain, probs, w_val, w_dir, w_out, curvature)[None]
    vm = functools.partial(pl.BlockSpec, memory_space=pltpu.VMEM)
    hbm = functools.partial(pl.BlockSpec, memory_space=pl.ANY)
    if fused:
        outs = jax.ShapeDtypeStruct((feats, hf), F32)
        out_specs = vm()
    else:
        outs = (jax.ShapeDtypeStruct((tok, width), BF), jax.ShapeDtypeStruct((tok, hf), BF))
        out_specs = (vm(), vm())
    sem = pltpu.SemaphoreType.DMA
    wide = N if fused else 1
    scratch = [
        pltpu.VMEM((hf, width), BF),
        pltpu.VMEM((width, hf), BF),
        pltpu.VMEM((width, hf), BF),
        pltpu.VMEM((tok, width), BF),
        pltpu.VMEM((tok, hf), BF),
        pltpu.VMEM((tok, width), F32),
        pltpu.VMEM((tok, width), BF),
        pltpu.VMEM((T, rows, width), BF),
        pltpu.VMEM((T, rows, width), BF),
        pltpu.VMEM((T, rows, width), BF),
        pltpu.VMEM((tok, width), BF),
        pltpu.VMEM((tok, width), BF),
        pltpu.VMEM((tok, width), BF),
        pltpu.VMEM((tok, width), BF),
        pltpu.VMEM((rows, width), F32),
        pltpu.VMEM((rows, width), BF),
        pltpu.VMEM((wide, tok, hf), BF),
        pltpu.VMEM((wide, tok, feats if fused else 128), BF),
        sem((4,)),
        sem((N,)), sem((N,)),
        sem((T,)), sem((T,)),
        sem((T,)), sem((T,)),
        sem((T,)), sem((T,)),
        sem((T,)), sem((T,)),
        sem((T,)), sem((T,)),
        sem((wide, T)), sem((wide, T)),
        sem((N,)), sem((N,)),
    ]
    result = pl.pallas_call(
        functools.partial(kernel, fused, S, T, N),
        out_shape=outs,
        in_specs=[vm(), vm(), vm(), hbm(), hbm(), hbm(), hbm()],
        out_specs=out_specs,
        scratch_shapes=scratch,
        compiler_params=pltpu.CompilerParams(
            collective_id=0, has_side_effects=True, vmem_limit_bytes=56 * 1024 * 1024
        ),
    )(x, norm_gain, probs, w_val, w_dir, w_out, curvature)
    if fused:
        return result[None]
    adjoint, act = result
    product = lax.psum_scatter(
        dot_tn(adjoint, act).astype(BF), "dp", scatter_dimension=0, tiled=True
    ).astype(F32)
    return product[None]


def solution(mesh):
    in_specs = (
        P("section", "dp", None),
        P("section", None),
        P("section", "tensor", None),
        P("section", "tensor", "dp", None),
        P("section", None, "tensor"),
        P("section", None, "tensor"),
        P("dp", None),
    )
    out_specs = P("section", "dp", "tensor")
    return jax.shard_map(
        per_device, mesh=mesh, in_specs=in_specs, out_specs=out_specs, check_vma=False
    )
```
